256 devices in a mesh: seq: 32 (over y, z), tensor: 8 (over x, core).
Axes of the slice: x: 4, y: 4, z: 8, core: 2. Of those that a mesh axis runs over, the one named last changes fastest.
Arguments:
- hidden: bfloat16 [8192, 2048], P(('seq', 'tensor')), may hold values from -6 to 6
- attn_gain: float32 [2048], replicated, may hold values from 0.25 to 1.75
- attn_query: bfloat16 [2048, 2048], P(None, 'tensor'), may hold values from -0.015625 to 0.015625
- attn_key: bfloat16 [2048, 2048], P(None, 'tensor'), may hold values from -0.125 to 0.125
- attn_value: bfloat16 [2048, 2048], P(None, 'tensor'), may hold values from -0.125 to 0.125
- attn_out: bfloat16 [2048, 2048], P('tensor'), may hold values from -0.125 to 0.125
- ff_gain: float32 [2048], replicated, may hold values from 0.25 to 1.75
- ff_gate: bfloat16 [2048, 5120], P(None, 'tensor'), may hold values from -0.125 to 0.125
- ff_up: bfloat16 [2048, 5120], P(None, 'tensor'), may hold values from -0.125 to 0.125
- ff_down: bfloat16 [5120, 2048], P('tensor'), may hold values from -0.078125 to 0.078125
- final_gain: float32 [2048], replicated, may hold values from 0.25 to 1.75
- embedding: bfloat16 [32128, 2048], P('seq', 'tensor'), may hold values from -0.375 to 0.375
- rel_weight: float32 [32, 32], P(None, 'tensor'), may hold values from -6 to 6
- bucket_table: int32 [2048], replicated, may hold values from 0 to 31
- prefix_kv: bfloat16 [2, 32, 256, 2048], P(None, 'seq', None, 'tensor'), may hold values from -1600 to 1600, as said below
- node_lengths: int32 [32], replicated, may hold values from 1 to 256, 3072 in all
- group_branch: int32 [24], replicated, may hold values from 0 to 6
- node_slot: int32 [32], replicated, may hold values from 0 to 31, each once
- request_group: int32 [32], replicated, may hold values from 0 to 23
Outputs:
- hidden_out: bfloat16 [8192, 2048], P(('seq', 'tensor'))
- last_rms: float32 [32], replicated
- top_logit: float32 [32], replicated
The draws below stay inside these ranges and needn't reach their ends.
Inputs may be any that keep to these rules, and one draw needn't show every extreme that they name: `prefix_kv`: finite entries.
All inputs are finite; a program needn't handle non-finite values.
Results may differ from the reference program's by a relative error of at most 0.018.
The reference program's roundings to bfloat16 on the way count: a program that leaves them out, or rounds other values in their place, can miss the bound.
Values may be sent and summed in bfloat16 or wider, within the bound.
A program may use at most 192 MiB of HBM per device.

```python
import math
import jax
import jax.numpy as jnp
import numpy as np
from jax import lax

D = 2048
HEADS = 32
DH = 64
FF = 5120
VOCAB = 32128
NB = 32
SUF = 256
CAP = 256
BRANCHES = 7
GROUPS = 24
NODES = 32
REQUESTS = 32
TOKENS = 8192
RELS = 2048


def draw_prefix_kv(key, part):
    shape_all = (2, NODES, CAP, HEADS * DH)
    return jnp.clip(jax.random.normal(key, shape_all, jnp.float32), -6.0, 6.0).astype(jnp.bfloat16)


def plant(drawn, own_key, least, largest):
    place = [jax.random.randint(jax.random.fold_in(own_key, axis), (), 0, length) for axis, length in enumerate(drawn.shape)]
    longest = drawn.shape.index(max(drawn.shape))
    beside = place[:longest] + [(place[longest] + 1) % drawn.shape[longest]] + place[longest + 1:]
    return drawn.at[tuple(place)].set(least).at[tuple(beside)].set(largest)


def level_of(own_key, shape, shards, smallest, high):
    def one(axis_at, blocks):
        draws = jax.random.uniform(jax.random.fold_in(jax.random.fold_in(own_key, 6), axis_at), (blocks,), jnp.float32, smallest / len(shards), high / len(shards))
        return jnp.repeat(jnp.exp(draws), shape[axis_at] // blocks).reshape((-1,) + (1,) * (len(shape) - axis_at - 1))

    loudness = one(*shards[0])
    for cut in shards[1:]:
        loudness = loudness * one(*cut)
    return loudness


def split_up(count, total, reach, lean):
    portions = [(1 << 20) // math.isqrt(grade ** lean) + 1 for grade in range(2, count + 1)]
    surplus, given = total - reach - (count - 1), [1] * (count - 1)
    while surplus > 0:
        movable = [i for i in range(count - 1) if given[i] < reach]
        mass, left = sum([portions[i] for i in movable]), surplus
        for i in movable:
            more = min(reach - given[i], max(1, left * portions[i] // mass), surplus)
            given[i] = given[i] + more
            surplus = surplus - more
    return np.array([reach] + given)


def uneven(stream_key, number_of, total, limit, lean):
    if number_of == 2:
        one = jax.random.randint(stream_key, (), max(1, total - limit), min(limit, total - 1) + 1)
        return jnp.stack([one, total - one])
    tallies = jnp.asarray(split_up(number_of, total, limit, lean), jnp.int32)
    pairs = (number_of - 1) // 2
    giver, sink = tallies[1:1 + 2 * pairs:2], tallies[2:2 + 2 * pairs:2]
    margin = jnp.minimum(giver - 1, limit - sink)
    moved = jax.random.randint(jax.random.fold_in(stream_key, 1), (pairs,), 0, 1 << 20) % (margin + 1)
    tallies = tallies.at[1:1 + 2 * pairs:2].set(giver - moved).at[2:2 + 2 * pairs:2].set(sink + moved)
    return tallies[jax.random.permutation(jax.random.fold_in(stream_key, 2), number_of)]


def gaussian(key, shape, spread, limit, pieces=(), kind=jnp.bfloat16):
    values = spread * jax.random.normal(key, shape, jnp.float32)
    if pieces:
        values = values * level_of(key, shape, pieces, -0.22, 0.18)
    return jnp.clip(values, -limit, limit).astype(kind)


def setup_inputs(seed: int = 0) -> dict:
    streams_of = jax.random.split(jax.random.key(seed), 20)
    return {
        "hidden": gaussian(streams_of[0], (TOKENS, D), 1.0, 6.0, ((0, 256),)),
        "attn_gain": jnp.clip(1.0 + 0.15 * jax.random.normal(streams_of[1], (D,), jnp.float32), 0.25, 1.75),
        "attn_query": gaussian(streams_of[2], (D, HEADS * DH), (D * DH) ** -0.5, 0.015625, ((1, 8),)),
        "attn_key": gaussian(streams_of[3], (D, HEADS * DH), D ** -0.5, 0.125, ((1, 8),)),
        "attn_value": gaussian(streams_of[4], (D, HEADS * DH), D ** -0.5, 0.125, ((1, 8),)),
        "attn_out": gaussian(streams_of[5], (HEADS * DH, D), (HEADS * DH) ** -0.5, 0.125, ((0, 8),)),
        "ff_gain": jnp.clip(1.0 + 0.15 * jax.random.normal(streams_of[6], (D,), jnp.float32), 0.25, 1.75),
        "ff_gate": gaussian(streams_of[7], (D, FF), D ** -0.5, 0.125, ((1, 8),)),
        "ff_up": gaussian(streams_of[8], (D, FF), D ** -0.5, 0.125, ((1, 8),)),
        "ff_down": gaussian(streams_of[9], (FF, D), FF ** -0.5, 0.078125, ((0, 8),)),
        "final_gain": jnp.clip(1.0 + 0.15 * jax.random.normal(streams_of[10], (D,), jnp.float32), 0.25, 1.75),
        "embedding": gaussian(streams_of[11], (VOCAB, D), (D // 9) ** -0.5, 0.375, ((0, 32), (1, 8))),
        "rel_weight": gaussian(streams_of[12], (NB, HEADS), 1.0, 6.0, ((1, 8),), jnp.float32),
        "bucket_table": plant(jax.random.randint(streams_of[13], (RELS,), 0, NB), jax.random.fold_in(streams_of[13], 1), 0, NB - 1).astype(jnp.int32),
        "prefix_kv": draw_prefix_kv(jax.random.fold_in(streams_of[19], 71), 0),
        "node_lengths": uneven(streams_of[15], NODES, 12 * CAP, CAP, 2).astype(jnp.int32),
        "group_branch": plant(jax.random.randint(streams_of[16], (GROUPS,), 0, BRANCHES), jax.random.fold_in(streams_of[16], 1), 0, BRANCHES - 1).astype(jnp.int32),
        "node_slot": jax.random.permutation(streams_of[17], NODES).astype(jnp.int32),
        "request_group": plant(jax.random.randint(streams_of[18], (REQUESTS,), 0, GROUPS), jax.random.fold_in(streams_of[18], 1), 0, GROUPS - 1).astype(jnp.int32),
    }


def rms_scale(values, gain):
    widened = values.astype(jnp.float32)
    mean_square = lax.optimization_barrier(jnp.mean(widened * widened, axis=-1, keepdims=True))
    return widened * lax.rsqrt(mean_square + 1e-06) * gain

def attend(queries, key_rows, value_rows, table_bias, query_base, key_start, key_count):
    query_count = queries.shape[0]
    key_span = key_rows.shape[0]
    offset = table_bias.shape[1] // 2
    first_col = (offset + key_start - query_base - (query_count - 1)).astype(jnp.int32)
    bias_slab = lax.dynamic_slice_in_dim(table_bias, first_col, key_span + query_count - 1, 1)
    lookup = jnp.arange(key_span)[None, :] - jnp.arange(query_count)[:, None] + (query_count - 1)
    bias_block = jnp.take(bias_slab, lookup, axis=1)
    scores = jnp.einsum('qhe,khe->hqk', queries.astype(jnp.float32), key_rows.astype(jnp.float32)) + bias_block
    is_valid = jnp.arange(key_span) < key_count
    scores = jnp.where(is_valid[None, None, :], scores, -1e+30)
    row_peak = lax.optimization_barrier(jnp.max(scores, axis=2))
    weights = jnp.exp(scores - row_peak[:, :, None])
    row_total = lax.optimization_barrier(jnp.sum(weights, axis=2))
    rounded = lax.optimization_barrier(weights.astype(jnp.bfloat16))
    weighted = jnp.einsum('hqk,khe->qhe', rounded.astype(jnp.float32), value_rows.astype(jnp.float32))
    output = (weighted / jnp.transpose(row_total)[:, :, None]).astype(jnp.bfloat16)
    return (output, jnp.transpose(row_peak), jnp.transpose(row_total))

def combine_parts(outputs, peaks, totals):
    highest = lax.optimization_barrier(jnp.max(peaks, axis=0, keepdims=True))
    scales = totals * jnp.exp(peaks - highest)
    numer = lax.optimization_barrier(jnp.sum(scales[..., None] * outputs.astype(jnp.float32), axis=0))
    return numer / lax.optimization_barrier(jnp.sum(scales, axis=0))[..., None]

def reference(hidden, attn_gain, attn_query, attn_key, attn_value, attn_out, ff_gain, ff_gate, ff_up, ff_down, final_gain, embedding, rel_weight, bucket_table, prefix_kv, node_lengths, group_branch, node_slot, request_group):
    normed = rms_scale(hidden, attn_gain).astype(jnp.bfloat16)
    query_all = jnp.dot(normed, attn_query, preferred_element_type=jnp.float32).astype(jnp.bfloat16)
    key_all = jnp.dot(normed, attn_key, preferred_element_type=jnp.float32).astype(jnp.bfloat16)
    value_all = jnp.dot(normed, attn_value, preferred_element_type=jnp.float32).astype(jnp.bfloat16)
    table_bias = jnp.transpose(rel_weight[bucket_table])
    shaped = (REQUESTS, SUF, HEADS, DH)
    query_req = query_all.reshape(shaped)
    key_req = key_all.reshape(shaped)
    value_req = value_all.reshape(shaped)

    def per_request(request):
        group_id = request_group[request]
        branch = 1 + group_branch[group_id]
        group_node = 1 + BRANCHES + group_id
        path_nodes = jnp.stack([jnp.zeros_like(group_id), branch, group_node])
        path_counts = node_lengths[path_nodes]
        path_starts = jnp.stack([jnp.zeros_like(path_counts[0]), path_counts[0], path_counts[0] + path_counts[1]])
        base_pos = jnp.sum(path_counts)
        own_query = query_req[request]
        part_outs = []
        part_peaks = []
        part_totals = []
        for level_idx in range(3):
            slot_kv = prefix_kv[:, node_slot[path_nodes[level_idx]]]
            cache_keys = slot_kv[0].reshape(CAP, HEADS, DH)
            cache_values = slot_kv[1].reshape(CAP, HEADS, DH)
            output, row_peak, row_total = attend(own_query, cache_keys, cache_values, table_bias, base_pos, path_starts[level_idx], path_counts[level_idx])
            part_outs.append(output)
            part_peaks.append(row_peak)
            part_totals.append(row_total)
        output, row_peak, row_total = attend(own_query, key_req[request], value_req[request], table_bias, base_pos, base_pos, SUF)
        part_outs.append(output)
        part_peaks.append(row_peak)
        part_totals.append(row_total)
        merged = combine_parts(jnp.stack(part_outs), jnp.stack(part_peaks), jnp.stack(part_totals))
        return merged.astype(jnp.bfloat16).reshape(SUF, HEADS * DH)
    attn = lax.map(per_request, jnp.arange(REQUESTS)).reshape(TOKENS, HEADS * DH)
    mid = (hidden.astype(jnp.float32) + jnp.dot(attn, attn_out, preferred_element_type=jnp.float32)).astype(jnp.bfloat16)
    normed_mid = rms_scale(mid, ff_gain).astype(jnp.bfloat16)
    gate_part = jnp.dot(normed_mid, ff_gate, preferred_element_type=jnp.float32)
    up_part = jnp.dot(normed_mid, ff_up, preferred_element_type=jnp.float32)
    inner = (jax.nn.gelu(gate_part, approximate=True) * up_part).astype(jnp.bfloat16)
    hidden_out = (mid.astype(jnp.float32) + jnp.dot(inner, ff_down, preferred_element_type=jnp.float32)).astype(jnp.bfloat16)
    last_rows = hidden_out[SUF - 1::SUF].astype(jnp.float32)
    mean_square = lax.optimization_barrier(jnp.mean(last_rows * last_rows, axis=1))
    last_rms = jnp.sqrt(mean_square)
    final_rows = (last_rows * lax.rsqrt(mean_square + 1e-06)[:, None] * final_gain).astype(jnp.bfloat16)
    logits = jnp.dot(final_rows, jnp.transpose(embedding), preferred_element_type=jnp.float32)
    top_logit = lax.optimization_barrier(jnp.max(logits, axis=1))
    return (hidden_out, last_rms, top_logit)
```

```python
import functools

import jax
import jax.numpy as jnp
from jax import lax
from jax.experimental import pallas as pl
from jax.experimental.pallas import tpu as pltpu
from jax.sharding import PartitionSpec as P

MESH = pl.DeviceIdType.MESH
BRANCHES = 7
EPS = 1e-06
MASKED = -1e30
F32 = jnp.float32
BF16 = jnp.bfloat16
NT = (((1,), (1,)), ((), ()))


def remote(src, dst, send_sem, recv_sem, **device):
    return pltpu.make_async_remote_copy(
        src_ref=src, dst_ref=dst, send_sem=send_sem, recv_sem=recv_sem, device_id=device, device_id_type=MESH
    )


def dot(a, b):
    return jnp.dot(a, b, preferred_element_type=F32)


def rms_scale(values, gain):
    mean_square = jnp.mean(values * values, axis=-1, keepdims=True)
    return (values * lax.rsqrt(mean_square + EPS) * gain).astype(BF16)


def kernel(
    ns,
    nt,
    node_lengths,
    group_branch,
    node_slot,
    request_group,
    rel_weight,
    hidden,
    attn_gain,
    ff_gain,
    final_gain,
    bucket_table,
    kv_in,
    wq_in,
    wk_in,
    wv_in,
    wo_in,
    wg_in,
    wu_in,
    wd_in,
    emb_in,
    out,
    misc,
    wq,
    wk,
    wv,
    wo,
    wg,
    wu,
    wd,
    emb,
    full1,
    full2,
    slots,
    kv_send,
    path_kv,
    bias,
    query,
    own_key,
    own_value,
    attn,
    inner_rows,
    half_send1,
    half_recv1,
    part_send1,
    part_recv1,
    half_send2,
    half_recv2,
    part_send2,
    part_recv2,
    own_sum,
    last_send,
    last_mine,
    last_all,
    logit_send,
    logit_all,
    top_t,
    top_s,
    wsem,
    ag_send,
    ag_recv,
    rs_send,
    rs_recv,
    seq_send,
    seq_recv,
    tail_send,
    tail_recv,
):
    nx = nt // 2
    nz = 8 if ns % 8 == 0 else ns
    ny = ns // nz
    me_s = lax.axis_index("seq")
    me_t = lax.axis_index("tensor")
    x, core = me_t // 2, me_t % 2
    y, z = me_s // nz, me_s % nz
    sibling = me_t + 1 - 2 * core
    rows, width = hidden.shape
    suf = rows * nt
    heads = rel_weight.shape[1]
    cols = wq.shape[1]
    chunk = kv_in.shape[1]
    cap = chunk * ns // 2

    def seq_peer(k):
        return ((y + k // nz) % ny) * nz + (z + k % nz) % nz

    def seq_from(k):
        return ((y + ny - k // nz) % ny) * nz + (z + nz - k % nz) % nz

    weights = [(wq_in, wq), (wk_in, wk), (wv_in, wv), (wo_in, wo), (wg_in, wg), (wu_in, wu), (wd_in, wd), (emb_in, emb)]
    loads = [pltpu.make_async_copy(a, b, wsem.at[i]) for i, (a, b) in enumerate(weights)]
    own_slot = pltpu.make_async_copy(kv_in.at[me_s], slots.at[me_s], wsem.at[len(weights)])
    own_slot.start()
    for load in loads:
        load.start()

    barrier = pltpu.get_barrier_semaphore()

    @pl.loop(1, ns)
    def _(k):
        pl.semaphore_signal(barrier, inc=1, device_id={"seq": seq_peer(k)}, device_id_type=MESH)

    for k in range(1, nt):
        pl.semaphore_signal(barrier, inc=1, device_id={"tensor": (me_t + k) % nt}, device_id_type=MESH)

    full1[me_t] = rms_scale(hidden[...].astype(F32), attn_gain[...])
    pl.semaphore_wait(barrier, ns - 1 + nt - 1)

    @pl.loop(1, ns)
    def _(k):
        peer = seq_peer(k)
        remote(kv_in.at[peer], slots.at[me_s], seq_send.at[0, k], seq_recv.at[0, me_s], seq=peer).start()

    def gather_start(buf, phase):
        copies = [remote(buf.at[me_t], buf.at[me_t], ag_send.at[phase, 0], ag_recv.at[phase, me_t], tensor=sibling)]
        for k in range(1, nx):
            peer = ((x + k) % nx) * 2 + core
            copies.append(remote(buf.at[me_t], buf.at[me_t], ag_send.at[phase, k], ag_recv.at[phase, me_t], tensor=peer))
        for copy in copies:
            copy.start()
        return copies

    def gather_finish(buf, phase, copies):
        for k in range(1, nx):
            block = ((x + nx - k) % nx) * 2 + core
            remote(buf.at[block], buf.at[block], ag_send.at[phase, nx], ag_recv.at[phase, block], tensor=sibling).wait_recv()
            copy = remote(
                buf.at[block], buf.at[block], ag_send.at[phase, nx - 1 + k], ag_recv.at[phase, block], tensor=sibling
            )
            copy.start()
            copies.append(copy)
        for k in range(nx):
            block = ((x + nx - k) % nx) * 2 + 1 - core
            remote(buf.at[block], buf.at[block], ag_send.at[phase, nx], ag_recv.at[phase, block], tensor=sibling).wait_recv()
        for copy in copies:
            copy.wait_send()
        return buf[...].reshape(suf, width)

    copies = gather_start(full1, 0)

    def path_of(request):
        group = request_group[request]
        return 0, 1 + group_branch[group], 1 + BRANCHES + group

    nodes = path_of(me_s)
    lengths = [node_lengths[n] for n in nodes]
    base = lengths[0] + lengths[1] + lengths[2]
    starts = [0, lengths[0], lengths[0] + lengths[1], base]

    rels = bucket_table.shape[1]
    table = jnp.broadcast_to(bucket_table[...], (8, rels))
    sub = lax.broadcasted_iota(jnp.int32, (8, 1), 0)
    head_bias = jnp.zeros((8, rels), F32)
    for b in range(rel_weight.shape[0]):
        column = jnp.zeros((8, 1), F32)
        for h in range(heads):
            column = jnp.where(sub == h, rel_weight[b, h], column)
        head_bias = jnp.where(table == b, column, head_bias)
    half = suf // 2
    span = 2 * suf
    for part in range(4):
        first = rels // 2 - suf + 1 + starts[part] - base
        slab = pltpu.roll(head_bias, rels - first, 1)[:, :span]
        for h in range(heads):
            spread = jnp.broadcast_to(slab[h : h + 1, :], (half, span))
            turned = pltpu.roll(spread, span - half + 1, 1, stride=1, stride_axis=0)
            bias[h, part] = turned[:, : span - half]

    @pl.loop(1, ns)
    def _(k):
        peer = seq_from(k)
        remote(kv_in.at[peer], slots.at[peer], seq_send.at[0, k], seq_recv.at[0, peer], seq=peer).wait_recv()

    own_slot.wait()

    @pl.loop(1, ns)
    def _(k):
        peer = seq_peer(k)
        for level, node in enumerate(path_of(peer)):
            kv_send[k, level] = slots[node_slot[node]]
        remote(kv_send.at[k], path_kv.at[:, me_s], seq_send.at[1, k], seq_recv.at[1, me_s], seq=peer).start()

    for level, node in enumerate(nodes):
        path_kv[level, me_s] = slots[node_slot[node]]

    all_rows = gather_finish(full1, 0, copies)
    for i, (weight, result) in enumerate(((wq, query), (wk, own_key), (wv, own_value))):
        loads[i].wait()
        result[...] = dot(all_rows, weight[...]).astype(BF16)

    @pl.loop(1, ns)
    def _(k):
        peer = seq_from(k)
        remote(kv_send.at[k], path_kv.at[:, peer], seq_send.at[1, k], seq_recv.at[1, peer], seq=peer).wait_recv()

    lane = lax.broadcasted_iota(jnp.int32, (1, cap), 1)
    penalty = [jnp.where(lane < lengths[level], 0.0, MASKED) for level in range(3)]
    pair_lane = lax.broadcasted_iota(jnp.int32, (1, 128), 1)
    per_pair = 128 // (cols // heads)
    half_chunks = ns // 2
    for pair in range(cols // 128):
        at = slice(pair * 128, pair * 128 + 128)
        keys = [path_kv[level, :half_chunks, :, at].reshape(cap, 128) for level in range(3)] + [own_key[:, at]]
        values = [path_kv[level, half_chunks:, :, at].reshape(cap, 128) for level in range(3)] + [own_value[:, at]]
        for block in range(2):
            pair_query = query[block * half : block * half + half, at]
            merged = None
            for e in range(per_pair):
                h = pair * per_pair + e
                mine = pair_lane // (128 // per_pair) == e
                head_query = jnp.where(mine, pair_query, jnp.zeros((), BF16))
                scores = []
                for part in range(4):
                    score = lax.dot_general(head_query, keys[part], NT, preferred_element_type=F32)
                    score = score + bias[h, part, :, half * (1 - block) : half * (1 - block) + suf]
                    scores.append(score + penalty[part] if part < 3 else score)
                peak = jnp.max(jnp.maximum(jnp.maximum(scores[0], scores[1]), jnp.maximum(scores[2], scores[3])), axis=1, keepdims=True)
                total = None
                summed = None
                for part in range(4):
                    prob = jnp.exp(scores[part] - peak)
                    total = prob if total is None else total + prob
                    term = dot(prob.astype(BF16), values[part])
                    summed = term if summed is None else summed + term
                head_out = summed / jnp.sum(total, axis=1, keepdims=True)
                merged = head_out if merged is None else jnp.where(mine, head_out, merged)
            merged = merged.astype(BF16)
            for r in range(half // rows):
                attn[block * (half // rows) + r, :, at] = merged[r * rows : r * rows + rows]

    def scatter_sum(left, weight, half_send, half_recv, part_send, part_recv, phase):
        def product(parity):
            picked = jnp.concatenate([left[2 * i + parity] for i in range(nx)], axis=0)
            return dot(picked, weight[...]).reshape(nx, rows, width)

        half_send[...] = product(1 - core).astype(BF16)
        over = remote(half_send, half_recv, rs_send.at[phase, 0], rs_recv.at[phase, nx], tensor=sibling)
        over.start()
        own_sum[...] = product(core)
        over.wait_recv()
        sent = [over]
        for k in range(1, nx):
            dest = (x + k) % nx
            part_send[k] = (own_sum[dest] + half_recv[dest].astype(F32)).astype(BF16)
            copy = remote(
                part_send.at[k], part_recv.at[x], rs_send.at[phase, k], rs_recv.at[phase, x], tensor=dest * 2 + core
            )
            copy.start()
            sent.append(copy)
        total = own_sum[x] + half_recv[x].astype(F32)
        for k in range(1, nx):
            source = (x + nx - k) % nx
            remote(
                part_send.at[k], part_recv.at[source], rs_send.at[phase, k], rs_recv.at[phase, source], tensor=sibling
            ).wait_recv()
            total = total + part_recv[source].astype(F32)
        for copy in sent:
            copy.wait_send()
        return total

    loads[3].wait()
    summed = scatter_sum(attn, wo, half_send1, half_recv1, part_send1, part_recv1, 0)
    mid = (hidden[...].astype(F32) + summed).astype(BF16).astype(F32)
    full2[me_t] = rms_scale(mid, ff_gain[...])
    copies = gather_start(full2, 1)
    all_rows = gather_finish(full2, 1, copies)
    loads[4].wait()
    loads[5].wait()
    gate = dot(all_rows, wg[...])
    up = dot(all_rows, wu[...])
    inner = (jax.nn.gelu(gate, approximate=True) * up).astype(BF16)
    inner_rows[...] = inner.reshape(nt, rows, inner.shape[1])
    loads[6].wait()
    total = scatter_sum(inner_rows, wd, half_send2, half_recv2, part_send2, part_recv2, 1)
    result = (mid + total).astype(BF16)
    out[...] = result

    last = result[rows - 1 : rows].astype(F32)
    mean_square = jnp.mean(last * last, axis=-1, keepdims=True)
    rms = jnp.broadcast_to(jnp.sqrt(mean_square), (1, 128))
    final = (last * lax.rsqrt(mean_square + EPS) * final_gain[...]).astype(BF16).astype(F32)
    for t in range(nt):
        last_send[t] = jnp.concatenate([final[:, t * cols : t * cols + cols], rms], axis=1)

    @pl.when(me_t == nt - 1)
    def _():
        sends = [
            remote(last_send.at[t], last_mine, tail_send.at[0, t], tail_recv.at[0, 0], tensor=t) for t in range(nt - 1)
        ]
        for send in sends:
            send.start()
        last_mine[...] = last_send[nt - 1]
        for send in sends:
            send.wait_send()

    @pl.when(me_t != nt - 1)
    def _():
        remote(last_send.at[0], last_mine, tail_send.at[0, 0], tail_recv.at[0, 0], tensor=sibling).wait_recv()

    @pl.loop(1, ns)
    def _(k):
        remote(last_mine, last_all.at[me_s], seq_send.at[2, k], seq_recv.at[2, me_s], seq=seq_peer(k)).start()

    last_all[me_s] = last_mine[...]
    loads[7].wait()

    @pl.loop(1, ns)
    def _(k):
        peer = seq_from(k)
        remote(last_mine, last_all.at[peer], seq_send.at[2, k], seq_recv.at[2, peer], seq=peer).wait_recv()

    lasts = last_all[...].reshape(ns, cols + 128)
    rms_all = lasts[:, cols:]
    vocab = emb.shape[0]
    logits = lax.dot_general(lasts[:, :cols].astype(BF16), emb[...], NT, preferred_element_type=F32)
    per = 128 * pl.cdiv(pl.cdiv(vocab, nt), 128)
    logits = jnp.concatenate([logits, jnp.full((ns, per * nt - vocab), MASKED, F32)], axis=1)
    for t in range(nt):
        logit_send[t] = logits[:, t * per : t * per + per]
    sends = []
    for k in range(1, nt):
        peer = (me_t + k) % nt
        send = remote(logit_send.at[peer], logit_all.at[me_t], tail_send.at[1, k], tail_recv.at[1, me_t], tensor=peer)
        send.start()
        sends.append(send)
    logit = logit_send[me_t]
    for k in range(1, nt):
        peer = (me_t + nt - k) % nt
        remote(logit_send.at[peer], logit_all.at[peer], tail_send.at[1, k], tail_recv.at[1, peer], tensor=peer).wait_recv()
        logit = logit + logit_all[peer]
    highest = jnp.max(logit, axis=1, keepdims=True)
    diagonal = lax.broadcasted_iota(jnp.int32, (ns, 128), 0) == lax.broadcasted_iota(jnp.int32, (ns, 128), 1)
    top_t[me_t] = jnp.max(jnp.where(diagonal, highest, 2 * nt * MASKED), axis=0, keepdims=True)
    for k in range(1, nt):
        peer = (me_t + k) % nt
        send = remote(top_t.at[me_t], top_t.at[me_t], tail_send.at[2, k], tail_recv.at[2, me_t], tensor=peer)
        send.start()
        sends.append(send)
    top = top_t[me_t]
    for k in range(1, nt):
        peer = (me_t + nt - k) % nt
        remote(top_t.at[peer], top_t.at[peer], tail_send.at[2, k], tail_recv.at[2, peer], tensor=peer).wait_recv()
        top = jnp.maximum(top, top_t[peer])
    top_s[me_s] = top

    @pl.loop(1, ns)
    def _(k):
        remote(top_s.at[me_s], top_s.at[me_s], seq_send.at[3, k], seq_recv.at[3, me_s], seq=seq_peer(k)).start()

    last_rms = jnp.sum(jnp.where(diagonal, rms_all, 0.0), axis=0, keepdims=True)

    @pl.loop(1, ns)
    def _(k):
        peer = seq_from(k)
        remote(top_s.at[peer], top_s.at[peer], seq_send.at[3, k], seq_recv.at[3, peer], seq=peer).wait_recv()

    top = jnp.max(top_s[...].reshape(ns, 128), axis=0, keepdims=True)
    misc[...] = jnp.concatenate([last_rms, top, jnp.zeros((6, 128), F32)], axis=0)

    for send in sends:
        send.wait_send()

    @pl.loop(1, ns)
    def _(k):
        peer = seq_peer(k)
        remote(kv_in.at[peer], slots.at[me_s], seq_send.at[0, k], seq_recv.at[0, me_s], seq=peer).wait_send()
        remote(kv_send.at[k], path_kv.at[:, me_s], seq_send.at[1, k], seq_recv.at[1, me_s], seq=peer).wait_send()
        remote(last_mine, last_all.at[me_s], seq_send.at[2, k], seq_recv.at[2, me_s], seq=peer).wait_send()
        remote(top_s.at[me_s], top_s.at[me_s], seq_send.at[3, k], seq_recv.at[3, me_s], seq=peer).wait_send()


def per_device(
    hidden,
    attn_gain,
    attn_query,
    attn_key,
    attn_value,
    attn_out,
    ff_gain,
    ff_gate,
    ff_up,
    ff_down,
    final_gain,
    embedding,
    rel_weight,
    bucket_table,
    prefix_kv,
    node_lengths,
    group_branch,
    node_slot,
    request_group,
):
    ns = lax.axis_size("seq")
    nt = lax.axis_size("tensor")
    nx = nt // 2
    rows, width = hidden.shape
    suf = rows * nt
    heads = rel_weight.shape[1]
    cols = attn_query.shape[1]
    cap = prefix_kv.shape[2]
    chunk = 2 * cap // ns
    per = 128 * pl.cdiv(pl.cdiv(embedding.shape[0], nt), 128)
    kv_chunks = prefix_kv.reshape(ns, chunk, cols)
    smem = pl.BlockSpec(memory_space=pltpu.SMEM)
    vmem = pl.BlockSpec(memory_space=pltpu.VMEM)
    hbm = pl.BlockSpec(memory_space=pl.ANY)
    weights = (attn_query, attn_key, attn_value, attn_out, ff_gate, ff_up, ff_down, embedding)
    dma = pltpu.SemaphoreType.DMA
    result, misc = pl.pallas_call(
        functools.partial(kernel, ns, nt),
        out_shape=(jax.ShapeDtypeStruct((rows, width), BF16), jax.ShapeDtypeStruct((8, 128), F32)),
        in_specs=[smem] * 5 + [vmem] * 5 + [hbm] * 9,
        out_specs=(vmem, vmem),
        scratch_shapes=[pltpu.VMEM(w.shape, BF16) for w in weights]
        + [
            pltpu.VMEM((nt, rows, width), BF16),
            pltpu.VMEM((nt, rows, width), BF16),
            pltpu.VMEM((ns, chunk, cols), BF16),
            pltpu.VMEM((ns, 3, chunk, cols), BF16),
            pltpu.VMEM((3, ns, chunk, cols), BF16),
            pltpu.VMEM((heads, 4, suf // 2, suf + suf // 2), F32),
            pltpu.VMEM((suf, cols), BF16),
            pltpu.VMEM((suf, cols), BF16),
            pltpu.VMEM((suf, cols), BF16),
            pltpu.VMEM((nt, rows, cols), BF16),
            pltpu.VMEM((nt, rows, ff_down.shape[0]), BF16),
        ]
        + [pltpu.VMEM((nx, rows, width), BF16) for _ in range(8)]
        + [
            pltpu.VMEM((nx, rows, width), F32),
            pltpu.VMEM((nt, 1, cols + 128), F32),
            pltpu.VMEM((1, cols + 128), F32),
            pltpu.VMEM((ns, 1, cols + 128), F32),
            pltpu.VMEM((nt, ns, per), F32),
            pltpu.VMEM((nt, ns, per), F32),
            pltpu.VMEM((nt, 1, 128), F32),
            pltpu.VMEM((ns, 1, 128), F32),
            dma((len(weights) + 1,)),
            dma((2, 2 * nx)),
            dma((2, nt)),
            dma((2, nx)),
            dma((2, nx + 1)),
            dma((4, ns)),
            dma((4, ns)),
            dma((3, nt)),
            dma((3, nt)),
        ],
        compiler_params=pltpu.CompilerParams(collective_id=0, has_side_effects=True, vmem_limit_bytes=60 << 20),
        name="layer",
    )(
        node_lengths,
        group_branch,
        node_slot,
        request_group,
        rel_weight,
        hidden,
        attn_gain.reshape(1, -1),
        ff_gain.reshape(1, -1),
        final_gain.reshape(1, -1),
        bucket_table.reshape(1, -1),
        kv_chunks,
        *weights,
    )
    return result, misc[0, :ns], misc[1, :ns]


def solution(mesh):
    return jax.shard_map(
        per_device,
        mesh=mesh,
        in_specs=(
            P(("seq", "tensor"), None),
            P(),
            P(None, "tensor"),
            P(None, "tensor"),
            P(None, "tensor"),
            P("tensor", None),
            P(),
            P(None, "tensor"),
            P(None, "tensor"),
            P("tensor", None),
            P(),
            P("seq", "tensor"),
            P(None, "tensor"),
            P(),
            P(None, "seq", None, "tensor"),
            P(),
            P(),
            P(),
            P(),
        ),
        out_specs=(P(("seq", "tensor"), None), P(), P()),
        check_vma=False,
    )
```

```python
import functools

import jax
import jax.numpy as jnp
from jax import lax
from jax.experimental import pallas as pl
from jax.experimental.pallas import tpu as pltpu
from jax.sharding import PartitionSpec as P

MESH = pl.DeviceIdType.MESH
BRANCHES = 7
EPS = 1e-06
MASKED = -1e30
F32 = jnp.float32
BF16 = jnp.bfloat16
NT = (((1,), (1,)), ((), ()))


def remote(src, dst, send_sem, recv_sem, **device):
    return pltpu.make_async_remote_copy(
        src_ref=src, dst_ref=dst, send_sem=send_sem, recv_sem=recv_sem, device_id=device, device_id_type=MESH
    )


def dot(a, b):
    return jnp.dot(a, b, preferred_element_type=F32)


def rms_scale(values, gain):
    mean_square = jnp.mean(values * values, axis=-1, keepdims=True)
    return (values * lax.rsqrt(mean_square + EPS) * gain).astype(BF16)


def kernel(
    ns,
    nt,
    node_lengths,
    group_branch,
    node_slot,
    request_group,
    rel_weight,
    hidden,
    attn_gain,
    ff_gain,
    final_gain,
    bucket_table,
    kv_in,
    wq_in,
    wk_in,
    wv_in,
    wo_in,
    wg_in,
    wu_in,
    wd_in,
    emb_in,
    out,
    misc,
    wq,
    wk,
    wv,
    wo,
    wg,
    wu,
    wd,
    emb,
    full1,
    full2,
    slots,
    kv_send,
    path_kv,
    bias,
    query,
    own_key,
    own_value,
    attn,
    inner_rows,
    half_send1,
    half_recv1,
    part_send1,
    part_recv1,
    half_send2,
    half_recv2,
    part_send2,
    part_recv2,
    own_sum,
    last_send,
    row_out,
    row_in,
    last_all,
    logit_send,
    logit_all,
    top_t,
    top_s,
    wsem,
    ag_send,
    ag_recv,
    rs_send,
    rs_recv,
    seq_send,
    seq_recv,
    tail_send,
    tail_recv,
):
    nx = nt // 2
    nz = 8 if ns % 8 == 0 else ns
    ny = ns // nz
    me_s = lax.axis_index("seq")
    me_t = lax.axis_index("tensor")
    x, core = me_t // 2, me_t % 2
    y, z = me_s // nz, me_s % nz
    sibling = me_t + 1 - 2 * core
    rows, width = hidden.shape
    suf = rows * nt
    heads = rel_weight.shape[1]
    cols = wq.shape[1]
    chunk = kv_in.shape[1]
    cap = chunk * ns // 2

    def seq_peer(k):
        return ((y + k // nz) % ny) * nz + (z + k % nz) % nz

    def seq_from(k):
        return ((y + ny - k // nz) % ny) * nz + (z + nz - k % nz) % nz

    weights = [(wq_in, wq), (wk_in, wk), (wv_in, wv), (wo_in, wo), (wg_in, wg), (wu_in, wu), (wd_in, wd), (emb_in, emb)]
    loads = [pltpu.make_async_copy(a, b, wsem.at[i]) for i, (a, b) in enumerate(weights)]
    own_slot = pltpu.make_async_copy(kv_in.at[me_s], slots.at[me_s], wsem.at[len(weights)])
    own_slot.start()
    for load in loads:
        load.start()

    barrier = pltpu.get_barrier_semaphore()

    @pl.loop(1, ns)
    def _(k):
        pl.semaphore_signal(barrier, inc=1, device_id={"seq": seq_peer(k)}, device_id_type=MESH)

    for k in range(1, nt):
        pl.semaphore_signal(barrier, inc=1, device_id={"tensor": (me_t + k) % nt}, device_id_type=MESH)

    full1[me_t] = rms_scale(hidden[...].astype(F32), attn_gain[...])
    pl.semaphore_wait(barrier, ns - 1 + nt - 1)

    @pl.loop(1, ns)
    def _(k):
        peer = seq_peer(k)
        remote(kv_in.at[peer], slots.at[me_s], seq_send.at[0, k], seq_recv.at[0, me_s], seq=peer).start()

    def gather_start(buf, phase):
        copies = [remote(buf.at[me_t], buf.at[me_t], ag_send.at[phase, 0], ag_recv.at[phase, me_t], tensor=sibling)]
        for k in range(1, nx):
            peer = ((x + k) % nx) * 2 + core
            copies.append(remote(buf.at[me_t], buf.at[me_t], ag_send.at[phase, k], ag_recv.at[phase, me_t], tensor=peer))
        for copy in copies:
            copy.start()
        return copies

    def gather_finish(buf, phase, copies):
        for k in range(1, nx):
            block = ((x + nx - k) % nx) * 2 + core
            remote(buf.at[block], buf.at[block], ag_send.at[phase, nx], ag_recv.at[phase, block], tensor=sibling).wait_recv()
            copy = remote(
                buf.at[block], buf.at[block], ag_send.at[phase, nx - 1 + k], ag_recv.at[phase, block], tensor=sibling
            )
            copy.start()
            copies.append(copy)
        for k in range(nx):
            block = ((x + nx - k) % nx) * 2 + 1 - core
            remote(buf.at[block], buf.at[block], ag_send.at[phase, nx], ag_recv.at[phase, block], tensor=sibling).wait_recv()
        for copy in copies:
            copy.wait_send()
        return buf[...].reshape(suf, width)

    copies = gather_start(full1, 0)

    def path_of(request):
        group = request_group[request]
        return 0, 1 + group_branch[group], 1 + BRANCHES + group

    nodes = path_of(me_s)
    lengths = [node_lengths[n] for n in nodes]
    base = lengths[0] + lengths[1] + lengths[2]
    starts = [0, lengths[0], lengths[0] + lengths[1], base]

    rels = bucket_table.shape[1]
    table = jnp.broadcast_to(bucket_table[...], (8, rels))
    sub = lax.broadcasted_iota(jnp.int32, (8, 1), 0)
    head_bias = jnp.zeros((8, rels), F32)
    for b in range(rel_weight.shape[0]):
        column = jnp.zeros((8, 1), F32)
        for h in range(heads):
            column = jnp.where(sub == h, rel_weight[b, h], column)
        head_bias = jnp.where(table == b, column, head_bias)
    half = suf // 2
    span = 2 * suf
    for part in range(4):
        first = rels // 2 - suf + 1 + starts[part] - base
        slab = pltpu.roll(head_bias, rels - first, 1)[:, :span]
        for h in range(heads):
            spread = jnp.broadcast_to(slab[h : h + 1, :], (half, span))
            turned = pltpu.roll(spread, span - half + 1, 1, stride=1, stride_axis=0)
            bias[h, part] = turned[:, : span - half]

    @pl.loop(1, ns)
    def _(k):
        peer = seq_from(k)
        remote(kv_in.at[peer], slots.at[peer], seq_send.at[0, k], seq_recv.at[0, peer], seq=peer).wait_recv()

    own_slot.wait()

    @pl.loop(1, ns)
    def _(k):
        peer = seq_peer(k)
        for level, node in enumerate(path_of(peer)):
            kv_send[k, level] = slots[node_slot[node]]
        remote(kv_send.at[k], path_kv.at[:, me_s], seq_send.at[1, k], seq_recv.at[1, me_s], seq=peer).start()

    for level, node in enumerate(nodes):
        path_kv[level, me_s] = slots[node_slot[node]]

    all_rows = gather_finish(full1, 0, copies)
    for i, (weight, result) in enumerate(((wq, query), (wk, own_key), (wv, own_value))):
        loads[i].wait()
        result[...] = dot(all_rows, weight[...]).astype(BF16)

    @pl.loop(1, ns)
    def _(k):
        peer = seq_from(k)
        remote(kv_send.at[k], path_kv.at[:, peer], seq_send.at[1, k], seq_recv.at[1, peer], seq=peer).wait_recv()

    lane = lax.broadcasted_iota(jnp.int32, (1, cap), 1)
    penalty = [jnp.where(lane < lengths[level], 0.0, MASKED) for level in range(3)]
    pair_lane = lax.broadcasted_iota(jnp.int32, (1, 128), 1)
    per_pair = 128 // (cols // heads)
    half_chunks = ns // 2
    for pair in range(cols // 128):
        at = slice(pair * 128, pair * 128 + 128)
        keys = [path_kv[level, :half_chunks, :, at].reshape(cap, 128) for level in range(3)] + [own_key[:, at]]
        values = [path_kv[level, half_chunks:, :, at].reshape(cap, 128) for level in range(3)] + [own_value[:, at]]
        for block in range(2):
            pair_query = query[block * half : block * half + half, at]
            merged = None
            for e in range(per_pair):
                h = pair * per_pair + e
                mine = pair_lane // (128 // per_pair) == e
                head_query = jnp.where(mine, pair_query, jnp.zeros((), BF16))
                scores = []
                for part in range(4):
                    score = lax.dot_general(head_query, keys[part], NT, preferred_element_type=F32)
                    score = score + bias[h, part, :, half * (1 - block) : half * (1 - block) + suf]
                    scores.append(score + penalty[part] if part < 3 else score)
                peak = jnp.max(jnp.maximum(jnp.maximum(scores[0], scores[1]), jnp.maximum(scores[2], scores[3])), axis=1, keepdims=True)
                total = None
                summed = None
                for part in range(4):
                    prob = jnp.exp(scores[part] - peak)
                    total = prob if total is None else total + prob
                    term = dot(prob.astype(BF16), values[part])
                    summed = term if summed is None else summed + term
                head_out = summed / jnp.sum(total, axis=1, keepdims=True)
                merged = head_out if merged is None else jnp.where(mine, head_out, merged)
            merged = merged.astype(BF16)
            for r in range(half // rows):
                attn[block * (half // rows) + r, :, at] = merged[r * rows : r * rows + rows]

    def row_send(row, phase):
        row_out[phase] = row
        for k in range(1, nt):
            peer = (me_t + k) % nt
            send = remote(
                row_out.at[phase], row_in.at[phase, me_t], tail_send.at[phase, k], tail_recv.at[phase, me_t], tensor=peer
            )
            send.start()
            sends.append(send)

    def row_sum(phase):
        row = row_out[phase]
        for k in range(1, nt):
            peer = (me_t + nt - k) % nt
            remote(
                row_out.at[phase], row_in.at[phase, peer], tail_send.at[phase, k], tail_recv.at[phase, peer], tensor=peer
            ).wait_recv()
            row = row + row_in[phase, peer]
        return row

    sends = []
    is_last = me_t == nt - 1

    def last_projected():
        row = dot(attn[nt - 1, rows - 16 : rows], wo[...])[15:16]
        row_send(row + jnp.where(is_last, hidden[rows - 1 : rows].astype(F32), 0.0), 0)

    def last_inner():
        row = row_sum(0).astype(BF16).astype(F32)
        left = jnp.broadcast_to(rms_scale(row, ff_gain[...]).astype(F32), (16, width)).astype(BF16)
        inner = (jax.nn.gelu(dot(left, wg[...]), approximate=True) * dot(left, wu[...])).astype(BF16)
        row_send(dot(inner, wd[...])[0:1] + jnp.where(is_last, row, 0.0), 1)

    def last_final():
        last = row_sum(1).astype(BF16).astype(F32)
        mean_square = jnp.mean(last * last, axis=-1, keepdims=True)
        rms = jnp.broadcast_to(jnp.sqrt(mean_square), (1, 128))
        final = (last * lax.rsqrt(mean_square + EPS) * final_gain[...]).astype(BF16).astype(F32)
        for t in range(nt):
            last_send[t] = jnp.concatenate([final[:, t * cols : t * cols + cols], rms], axis=1)

        @pl.loop(1, ns)
        def _(k):
            remote(
                last_send.at[me_t], last_all.at[me_s], seq_send.at[2, k], seq_recv.at[2, me_s], seq=seq_peer(k)
            ).start()

        last_all[me_s] = last_send[me_t]

    per = logit_send.shape[2]
    diagonal = lax.broadcasted_iota(jnp.int32, (ns, 128), 0) == lax.broadcasted_iota(jnp.int32, (ns, 128), 1)

    def last_logits():
        @pl.loop(1, ns)
        def _(k):
            peer = seq_from(k)
            remote(
                last_send.at[me_t], last_all.at[peer], seq_send.at[2, k], seq_recv.at[2, peer], seq=peer
            ).wait_recv()

        lasts = last_all[...].reshape(ns, cols + 128)
        vocab = emb.shape[0]
        logits = lax.dot_general(lasts[:, :cols].astype(BF16), emb[...], NT, preferred_element_type=F32)
        logits = jnp.concatenate([logits, jnp.full((ns, per * nt - vocab), MASKED, F32)], axis=1)
        for t in range(nt):
            logit_send[t] = logits[:, t * per : t * per + per]
        for k in range(1, nt):
            peer = (me_t + k) % nt
            send = remote(logit_send.at[peer], logit_all.at[me_t], tail_send.at[2, k], tail_recv.at[2, me_t], tensor=peer)
            send.start()
            sends.append(send)
        misc[0:1] = jnp.sum(jnp.where(diagonal, lasts[:, cols:], 0.0), axis=0, keepdims=True)

    def top_of_words():
        logit = logit_send[me_t]
        for k in range(1, nt):
            peer = (me_t + nt - k) % nt
            remote(
                logit_send.at[peer], logit_all.at[peer], tail_send.at[2, k], tail_recv.at[2, peer], tensor=peer
            ).wait_recv()
            logit = logit + logit_all[peer]
        highest = jnp.max(logit, axis=1, keepdims=True)
        top_t[me_t] = jnp.max(jnp.where(diagonal, highest, 2 * nt * MASKED), axis=0, keepdims=True)
        for k in range(1, nt):
            peer = (me_t + k) % nt
            send = remote(top_t.at[me_t], top_t.at[me_t], tail_send.at[3, k], tail_recv.at[3, me_t], tensor=peer)
            send.start()
            sends.append(send)

    def top_of_group():
        top = top_t[me_t]
        for k in range(1, nt):
            peer = (me_t + nt - k) % nt
            remote(top_t.at[peer], top_t.at[peer], tail_send.at[3, k], tail_recv.at[3, peer], tensor=peer).wait_recv()
            top = jnp.maximum(top, top_t[peer])
        top_s[me_s] = top

        @pl.loop(1, ns)
        def _(k):
            remote(top_s.at[me_s], top_s.at[me_s], seq_send.at[3, k], seq_recv.at[3, me_s], seq=seq_peer(k)).start()

    def top_of_all():
        @pl.loop(1, ns)
        def _(k):
            peer = seq_from(k)
            remote(top_s.at[peer], top_s.at[peer], seq_send.at[3, k], seq_recv.at[3, peer], seq=peer).wait_recv()

        misc[1:2] = jnp.max(top_s[...].reshape(ns, 128), axis=0, keepdims=True)

    def scatter_sum(left, weight, half_send, half_recv, part_send, part_recv, phase, early, late):
        def product(parity):
            picked = jnp.concatenate([left[2 * i + parity] for i in range(nx)], axis=0)
            return dot(picked, weight[...]).reshape(nx, rows, width)

        half_send[...] = product(1 - core).astype(BF16)
        over = remote(half_send, half_recv, rs_send.at[phase, 0], rs_recv.at[phase, nx], tensor=sibling)
        over.start()
        own_sum[...] = product(core)
        early()
        over.wait_recv()
        sent = [over]
        for k in range(1, nx):
            dest = (x + k) % nx
            part_send[k] = (own_sum[dest] + half_recv[dest].astype(F32)).astype(BF16)
            copy = remote(
                part_send.at[k], part_recv.at[x], rs_send.at[phase, k], rs_recv.at[phase, x], tensor=dest * 2 + core
            )
            copy.start()
            sent.append(copy)
        total = own_sum[x] + half_recv[x].astype(F32)
        late()
        for k in range(1, nx):
            source = (x + nx - k) % nx
            remote(
                part_send.at[k], part_recv.at[source], rs_send.at[phase, k], rs_recv.at[phase, source], tensor=sibling
            ).wait_recv()
            total = total + part_recv[source].astype(F32)
        for copy in sent:
            copy.wait_send()
        return total

    for i in range(3, 8):
        loads[i].wait()
    last_projected()
    summed = scatter_sum(attn, wo, half_send1, half_recv1, part_send1, part_recv1, 0, lambda: None, last_inner)
    mid = (hidden[...].astype(F32) + summed).astype(BF16).astype(F32)
    full2[me_t] = rms_scale(mid, ff_gain[...])
    copies = gather_start(full2, 1)
    last_final()
    all_rows = gather_finish(full2, 1, copies)
    last_logits()
    gate = dot(all_rows, wg[...])
    up = dot(all_rows, wu[...])
    inner = (jax.nn.gelu(gate, approximate=True) * up).astype(BF16)
    inner_rows[...] = inner.reshape(nt, rows, inner.shape[1])
    top_of_words()
    total = scatter_sum(inner_rows, wd, half_send2, half_recv2, part_send2, part_recv2, 1, top_of_group, lambda: None)
    result = (mid + total).astype(BF16)
    out[...] = result

    top_of_all()
    for send in sends:
        send.wait_send()

    @pl.loop(1, ns)
    def _(k):
        peer = seq_peer(k)
        remote(kv_in.at[peer], slots.at[me_s], seq_send.at[0, k], seq_recv.at[0, me_s], seq=peer).wait_send()
        remote(kv_send.at[k], path_kv.at[:, me_s], seq_send.at[1, k], seq_recv.at[1, me_s], seq=peer).wait_send()
        remote(last_send.at[me_t], last_all.at[me_s], seq_send.at[2, k], seq_recv.at[2, me_s], seq=peer).wait_send()
        remote(top_s.at[me_s], top_s.at[me_s], seq_send.at[3, k], seq_recv.at[3, me_s], seq=peer).wait_send()


def per_device(
    hidden,
    attn_gain,
    attn_query,
    attn_key,
    attn_value,
    attn_out,
    ff_gain,
    ff_gate,
    ff_up,
    ff_down,
    final_gain,
    embedding,
    rel_weight,
    bucket_table,
    prefix_kv,
    node_lengths,
    group_branch,
    node_slot,
    request_group,
):
    ns = lax.axis_size("seq")
    nt = lax.axis_size("tensor")
    nx = nt // 2
    rows, width = hidden.shape
    suf = rows * nt
    heads = rel_weight.shape[1]
    cols = attn_query.shape[1]
    cap = prefix_kv.shape[2]
    chunk = 2 * cap // ns
    per = 128 * pl.cdiv(pl.cdiv(embedding.shape[0], nt), 128)
    kv_chunks = prefix_kv.reshape(ns, chunk, cols)
    smem = pl.BlockSpec(memory_space=pltpu.SMEM)
    vmem = pl.BlockSpec(memory_space=pltpu.VMEM)
    hbm = pl.BlockSpec(memory_space=pl.ANY)
    weights = (attn_query, attn_key, attn_value, attn_out, ff_gate, ff_up, ff_down, embedding)
    dma = pltpu.SemaphoreType.DMA
    result, misc = pl.pallas_call(
        functools.partial(kernel, ns, nt),
        out_shape=(jax.ShapeDtypeStruct((rows, width), BF16), jax.ShapeDtypeStruct((8, 128), F32)),
        in_specs=[smem] * 5 + [vmem] * 5 + [hbm] * 9,
        out_specs=(vmem, vmem),
        scratch_shapes=[pltpu.VMEM(w.shape, BF16) for w in weights]
        + [
            pltpu.VMEM((nt, rows, width), BF16),
            pltpu.VMEM((nt, rows, width), BF16),
            pltpu.VMEM((ns, chunk, cols), BF16),
            pltpu.VMEM((ns, 3, chunk, cols), BF16),
            pltpu.VMEM((3, ns, chunk, cols), BF16),
            pltpu.VMEM((heads, 4, suf // 2, suf + suf // 2), F32),
            pltpu.VMEM((suf, cols), BF16),
            pltpu.VMEM((suf, cols), BF16),
            pltpu.VMEM((suf, cols), BF16),
            pltpu.VMEM((nt, rows, cols), BF16),
            pltpu.VMEM((nt, rows, ff_down.shape[0]), BF16),
        ]
        + [pltpu.VMEM((nx, rows, width), BF16) for _ in range(8)]
        + [
            pltpu.VMEM((nx, rows, width), F32),
            pltpu.VMEM((nt, 1, cols + 128), F32),
            pltpu.VMEM((2, 1, width), F32),
            pltpu.VMEM((2, nt, 1, width), F32),
            pltpu.VMEM((ns, 1, cols + 128), F32),
            pltpu.VMEM((nt, ns, per), F32),
            pltpu.VMEM((nt, ns, per), F32),
            pltpu.VMEM((nt, 1, 128), F32),
            pltpu.VMEM((ns, 1, 128), F32),
            dma((len(weights) + 1,)),
            dma((2, 2 * nx)),
            dma((2, nt)),
            dma((2, nx)),
            dma((2, nx + 1)),
            dma((4, ns)),
            dma((4, ns)),
            dma((4, nt)),
            dma((4, nt)),
        ],
        compiler_params=pltpu.CompilerParams(collective_id=0, has_side_effects=True, vmem_limit_bytes=60 << 20),
        name="layer",
    )(
        node_lengths,
        group_branch,
        node_slot,
        request_group,
        rel_weight,
        hidden,
        attn_gain.reshape(1, -1),
        ff_gain.reshape(1, -1),
        final_gain.reshape(1, -1),
        bucket_table.reshape(1, -1),
        kv_chunks,
        *weights,
    )
    return result, misc[0, :ns], misc[1, :ns]


def solution(mesh):
    return jax.shard_map(
        per_device,
        mesh=mesh,
        in_specs=(
            P(("seq", "tensor"), None),
            P(),
            P(None, "tensor"),
            P(None, "tensor"),
            P(None, "tensor"),
            P("tensor", None),
            P(),
            P(None, "tensor"),
            P(None, "tensor"),
            P("tensor", None),
            P(),
            P("seq", "tensor"),
            P(None, "tensor"),
            P(),
            P(None, "seq", None, "tensor"),
            P(),
            P(),
            P(),
            P(),
        ),
        out_specs=(P(("seq", "tensor"), None), P(), P()),
        check_vma=False,
    )
```

```python
import functools

import jax
import jax.numpy as jnp
from jax import lax
from jax.experimental import pallas as pl
from jax.experimental.pallas import tpu as pltpu
from jax.sharding import PartitionSpec as P

MESH = pl.DeviceIdType.MESH
BRANCHES = 7
EPS = 1e-06
MASKED = -1e30
F32 = jnp.float32
BF16 = jnp.bfloat16
NT = (((1,), (1,)), ((), ()))


def remote(src, dst, send_sem, recv_sem, **device):
    return pltpu.make_async_remote_copy(
        src_ref=src, dst_ref=dst, send_sem=send_sem, recv_sem=recv_sem, device_id=device, device_id_type=MESH
    )


def dot(a, b):
    return jnp.dot(a, b, preferred_element_type=F32)


def rms_scale(values, gain):
    mean_square = jnp.mean(values * values, axis=-1, keepdims=True)
    return (values * lax.rsqrt(mean_square + EPS) * gain).astype(BF16)


def kernel(
    ns,
    nt,
    node_lengths,
    group_branch,
    node_slot,
    request_group,
    rel_weight,
    hidden,
    attn_gain,
    ff_gain,
    final_gain,
    bucket_table,
    kv_in,
    wq_in,
    wk_in,
    wv_in,
    wo_in,
    wg_in,
    wu_in,
    wd_in,
    emb_in,
    out,
    misc,
    wq,
    wk,
    wv,
    wo,
    wg,
    wu,
    wd,
    emb,
    full1,
    full2,
    slots,
    kv_send,
    kv_column,
    path_kv,
    bias,
    query,
    own_key,
    own_value,
    attn,
    inner_rows,
    half_send1,
    half_recv1,
    part_send1,
    part_recv1,
    half_send2,
    half_recv2,
    part_send2,
    part_recv2,
    own_sum,
    last_send,
    row_out,
    row_in,
    last_all,
    logit_send,
    logit_all,
    top_t,
    top_s,
    wsem,
    ag_send,
    ag_recv,
    rs_send,
    rs_recv,
    seq_send,
    seq_recv,
    z_send,
    z_recv,
    y_send,
    y_recv,
    tail_send,
    tail_recv,
):
    nx = nt // 2
    nz = 8 if ns % 8 == 0 else ns
    ny = ns // nz
    me_s = lax.axis_index("seq")
    me_t = lax.axis_index("tensor")
    x, core = me_t // 2, me_t % 2
    y, z = me_s // nz, me_s % nz
    sibling = me_t + 1 - 2 * core
    rows, width = hidden.shape
    suf = rows * nt
    heads, buckets = rel_weight.shape
    cols = wq.shape[1]
    chunk = kv_in.shape[1]
    cap = chunk * ns // 2

    def seq_peer(k):
        return ((y + k // nz) % ny) * nz + (z + k % nz) % nz

    def seq_from(k):
        return ((y + ny - k // nz) % ny) * nz + (z + nz - k % nz) % nz

    weights = [(wq_in, wq), (wk_in, wk), (wv_in, wv), (wo_in, wo), (wg_in, wg), (wu_in, wu), (wd_in, wd), (emb_in, emb)]
    loads = [pltpu.make_async_copy(a, b, wsem.at[i]) for i, (a, b) in enumerate(weights)]
    own_slot = pltpu.make_async_copy(kv_in.at[me_s], slots.at[me_s], wsem.at[len(weights)])
    own_slot.start()
    for load in loads:
        load.start()

    barrier = pltpu.get_barrier_semaphore()

    @pl.loop(1, ns)
    def _(k):
        pl.semaphore_signal(barrier, inc=1, device_id={"seq": seq_peer(k)}, device_id_type=MESH)

    for k in range(1, nt):
        pl.semaphore_signal(barrier, inc=1, device_id={"tensor": (me_t + k) % nt}, device_id_type=MESH)

    full1[me_t] = rms_scale(hidden[...].astype(F32), attn_gain[...])
    pl.semaphore_wait(barrier, ns - 1 + nt - 1)

    @pl.loop(1, ns)
    def _(k):
        peer = seq_peer(k)
        remote(kv_in.at[peer], slots.at[me_s], seq_send.at[0, k], seq_recv.at[0, me_s], seq=peer).start()

    def gather_start(buf, phase):
        copies = [remote(buf.at[me_t], buf.at[me_t], ag_send.at[phase, 0], ag_recv.at[phase, me_t], tensor=sibling)]
        for k in range(1, nx):
            peer = ((x + k) % nx) * 2 + core
            copies.append(remote(buf.at[me_t], buf.at[me_t], ag_send.at[phase, k], ag_recv.at[phase, me_t], tensor=peer))
        for copy in copies:
            copy.start()
        return copies

    def gather_finish(buf, phase, copies):
        for k in range(1, nx):
            block = ((x + nx - k) % nx) * 2 + core
            remote(buf.at[block], buf.at[block], ag_send.at[phase, nx], ag_recv.at[phase, block], tensor=sibling).wait_recv()
            copy = remote(
                buf.at[block], buf.at[block], ag_send.at[phase, nx - 1 + k], ag_recv.at[phase, block], tensor=sibling
            )
            copy.start()
            copies.append(copy)
        for k in range(nx):
            block = ((x + nx - k) % nx) * 2 + 1 - core
            remote(buf.at[block], buf.at[block], ag_send.at[phase, nx], ag_recv.at[phase, block], tensor=sibling).wait_recv()
        for copy in copies:
            copy.wait_send()
        return buf[...].reshape(suf, width)

    copies = gather_start(full1, 0)

    def path_of(request):
        group = request_group[request]
        return 0, 1 + group_branch[group], 1 + BRANCHES + group

    nodes = path_of(me_s)
    lengths = [node_lengths[n] for n in nodes]
    base = lengths[0] + lengths[1] + lengths[2]
    starts = [0, lengths[0], lengths[0] + lengths[1], base]

    rels = bucket_table.shape[1]
    table = jnp.broadcast_to(bucket_table[...], (8, rels))
    sub = lax.broadcasted_iota(jnp.int32, (8, 1), 0)
    head_bias = jnp.zeros((8, rels), F32)
    for b in range(buckets):
        column = jnp.zeros((8, 1), F32)
        for h in range(heads):
            column = jnp.where(sub == h, rel_weight[h, b], column)
        head_bias = jnp.where(table == b, column, head_bias)
    half = suf // 2
    span = 2 * suf
    for part in range(4):
        first = rels // 2 - suf + 1 + starts[part] - base
        slab = pltpu.roll(head_bias, rels - first, 1)[:, :span]
        for h in range(heads):
            spread = jnp.broadcast_to(slab[h : h + 1, :], (half, span))
            turned = pltpu.roll(spread, span - half + 1, 1, stride=1, stride_axis=0)
            bias[h, part] = turned[:, : span - half]

    @pl.loop(1, ns)
    def _(k):
        peer = seq_from(k)
        remote(kv_in.at[peer], slots.at[peer], seq_send.at[0, k], seq_recv.at[0, peer], seq=peer).wait_recv()

    own_slot.wait()

    def column_chunks(column, to):
        to[0] = slots[node_slot[0]]
        for row in range(ny):
            branch, lowest = path_of(row * nz + column)[1:]
            to[1 + 2 * row] = slots[node_slot[branch]]
            to[2 + 2 * row] = slots[node_slot[lowest]]

    def z_step(i):
        return (i // 2 + 1) * (1 - 2 * (i % 2))

    def over_z(i):
        column = (z + nz + z_step(i)) % nz
        return remote(
            kv_send.at[column], kv_column.at[z], z_send.at[i], z_recv.at[z], seq=y * nz + column
        )

    @pl.loop(0, nz - 1)
    def _(i):
        column = (z + nz + z_step(i)) % nz
        column_chunks(column, kv_send.at[column])
        over_z(i).start()

    def over_y(k, column):
        row = (y + k) % ny
        at = y * nz + column
        root = remote(
            kv_column.at[column, 0],
            path_kv.at[0, at],
            y_send.at[0, k, column],
            y_recv.at[0, at],
            seq=row * nz + z,
        )
        below = remote(
            kv_column.at[column, pl.ds(1 + 2 * row, 2)],
            path_kv.at[pl.ds(1, 2), at],
            y_send.at[1, k, column],
            y_recv.at[1, at],
            seq=row * nz + z,
        )
        return root, below

    def pass_on(column):
        for k in range(1, ny):
            for copy in over_y(k, column):
                copy.start()
        at = y * nz + column
        path_kv[0, at] = kv_column[column, 0]
        path_kv[1, at] = kv_column[column, 1 + 2 * y]
        path_kv[2, at] = kv_column[column, 2 + 2 * y]

    column_chunks(z, kv_column.at[z])
    pass_on(z)

    all_rows = gather_finish(full1, 0, copies)
    for i, (weight, result) in enumerate(((wq, query), (wk, own_key), (wv, own_value))):
        loads[i].wait()
        result[...] = dot(all_rows, weight[...]).astype(BF16)

    @pl.loop(0, nz - 1)
    def _(i):
        column = (z + nz - z_step(i)) % nz
        remote(
            kv_send.at[column], kv_column.at[column], z_send.at[i], z_recv.at[column], seq=y * nz + column
        ).wait_recv()
        pass_on(column)

    @pl.loop(0, nz)
    def _(column):
        for k in range(1, ny):
            row = (y + ny - k) % ny
            at = row * nz + column
            remote(
                kv_column.at[column, 0], path_kv.at[0, at], y_send.at[0, k, column], y_recv.at[0, at], seq=row * nz + z
            ).wait_recv()
            remote(
                kv_column.at[column, pl.ds(1, 2)],
                path_kv.at[pl.ds(1, 2), at],
                y_send.at[1, k, column],
                y_recv.at[1, at],
                seq=row * nz + z,
            ).wait_recv()

    lane = lax.broadcasted_iota(jnp.int32, (1, cap), 1)
    penalty = [jnp.where(lane < lengths[level], 0.0, MASKED) for level in range(3)]
    pair_lane = lax.broadcasted_iota(jnp.int32, (1, 128), 1)
    per_pair = 128 // (cols // heads)
    half_chunks = ns // 2
    for pair in range(cols // 128):
        at = slice(pair * 128, pair * 128 + 128)
        keys = [path_kv[level, :half_chunks, :, at].reshape(cap, 128) for level in range(3)] + [own_key[:, at]]
        values = [path_kv[level, half_chunks:, :, at].reshape(cap, 128) for level in range(3)] + [own_value[:, at]]
        for block in range(2):
            pair_query = query[block * half : block * half + half, at]
            merged = None
            for e in range(per_pair):
                h = pair * per_pair + e
                mine = pair_lane // (128 // per_pair) == e
                head_query = jnp.where(mine, pair_query, jnp.zeros((), BF16))
                scores = []
                for part in range(4):
                    score = lax.dot_general(head_query, keys[part], NT, preferred_element_type=F32)
                    score = score + bias[h, part, :, half * (1 - block) : half * (1 - block) + suf]
                    scores.append(score + penalty[part] if part < 3 else score)
                peak = jnp.max(jnp.maximum(jnp.maximum(scores[0], scores[1]), jnp.maximum(scores[2], scores[3])), axis=1, keepdims=True)
                total = None
                summed = None
                for part in range(4):
                    prob = jnp.exp(scores[part] - peak)
                    total = prob if total is None else total + prob
                    term = dot(prob.astype(BF16), values[part])
                    summed = term if summed is None else summed + term
                head_out = summed / jnp.sum(total, axis=1, keepdims=True)
                merged = head_out if merged is None else jnp.where(mine, head_out, merged)
            merged = merged.astype(BF16)
            for r in range(half // rows):
                attn[block * (half // rows) + r, :, at] = merged[r * rows : r * rows + rows]

    def row_send(row, phase):
        row_out[phase] = row
        for k in range(1, nt):
            peer = (me_t + k) % nt
            send = remote(
                row_out.at[phase], row_in.at[phase, me_t], tail_send.at[phase, k], tail_recv.at[phase, me_t], tensor=peer
            )
            send.start()
            sends.append(send)

    def row_sum(phase):
        row = row_out[phase]
        for k in range(1, nt):
            peer = (me_t + nt - k) % nt
            remote(
                row_out.at[phase], row_in.at[phase, peer], tail_send.at[phase, k], tail_recv.at[phase, peer], tensor=peer
            ).wait_recv()
            row = row + row_in[phase, peer]
        return row

    sends = []
    is_last = me_t == nt - 1

    def last_projected():
        row = dot(attn[nt - 1, rows - 16 : rows], wo[...])[15:16]
        row_send(row + jnp.where(is_last, hidden[rows - 1 : rows].astype(F32), 0.0), 0)

    def last_inner():
        row = row_sum(0).astype(BF16).astype(F32)
        left = jnp.broadcast_to(rms_scale(row, ff_gain[...]).astype(F32), (16, width)).astype(BF16)
        inner = (jax.nn.gelu(dot(left, wg[...]), approximate=True) * dot(left, wu[...])).astype(BF16)
        row_send(dot(inner, wd[...])[0:1] + jnp.where(is_last, row, 0.0), 1)

    def last_final():
        last = row_sum(1).astype(BF16).astype(F32)
        mean_square = jnp.mean(last * last, axis=-1, keepdims=True)
        rms = jnp.broadcast_to(jnp.sqrt(mean_square), (1, 128))
        final = (last * lax.rsqrt(mean_square + EPS) * final_gain[...]).astype(BF16).astype(F32)
        for t in range(nt):
            last_send[t] = jnp.concatenate([final[:, t * cols : t * cols + cols], rms], axis=1)

        @pl.loop(1, ns)
        def _(k):
            remote(
                last_send.at[me_t], last_all.at[me_s], seq_send.at[1, k], seq_recv.at[1, me_s], seq=seq_peer(k)
            ).start()

        last_all[me_s] = last_send[me_t]

    per = logit_send.shape[2]
    diagonal = lax.broadcasted_iota(jnp.int32, (ns, 128), 0) == lax.broadcasted_iota(jnp.int32, (ns, 128), 1)

    def last_logits():
        @pl.loop(1, ns)
        def _(k):
            peer = seq_from(k)
            remote(
                last_send.at[me_t], last_all.at[peer], seq_send.at[1, k], seq_recv.at[1, peer], seq=peer
            ).wait_recv()

        lasts = last_all[...].reshape(ns, cols + 128)
        vocab = emb.shape[0]
        logits = lax.dot_general(lasts[:, :cols].astype(BF16), emb[...], NT, preferred_element_type=F32)
        logits = jnp.concatenate([logits, jnp.full((ns, per * nt - vocab), MASKED, F32)], axis=1)
        for t in range(nt):
            logit_send[t] = logits[:, t * per : t * per + per]
        for k in range(1, nt):
            peer = (me_t + k) % nt
            send = remote(logit_send.at[peer], logit_all.at[me_t], tail_send.at[2, k], tail_recv.at[2, me_t], tensor=peer)
            send.start()
            sends.append(send)
        misc[0:1] = jnp.sum(jnp.where(diagonal, lasts[:, cols:], 0.0), axis=0, keepdims=True)

    def top_of_words():
        logit = logit_send[me_t]
        for k in range(1, nt):
            peer = (me_t + nt - k) % nt
            remote(
                logit_send.at[peer], logit_all.at[peer], tail_send.at[2, k], tail_recv.at[2, peer], tensor=peer
            ).wait_recv()
            logit = logit + logit_all[peer]
        highest = jnp.max(logit, axis=1, keepdims=True)
        top_t[me_t] = jnp.max(jnp.where(diagonal, highest, 2 * nt * MASKED), axis=0, keepdims=True)
        for k in range(1, nt):
            peer = (me_t + k) % nt
            send = remote(top_t.at[me_t], top_t.at[me_t], tail_send.at[3, k], tail_recv.at[3, me_t], tensor=peer)
            send.start()
            sends.append(send)

    def top_of_group():
        top = top_t[me_t]
        for k in range(1, nt):
            peer = (me_t + nt - k) % nt
            remote(top_t.at[peer], top_t.at[peer], tail_send.at[3, k], tail_recv.at[3, peer], tensor=peer).wait_recv()
            top = jnp.maximum(top, top_t[peer])
        top_s[me_s] = top

        @pl.loop(1, ns)
        def _(k):
            remote(top_s.at[me_s], top_s.at[me_s], seq_send.at[2, k], seq_recv.at[2, me_s], seq=seq_peer(k)).start()

    def top_of_all():
        @pl.loop(1, ns)
        def _(k):
            peer = seq_from(k)
            remote(top_s.at[peer], top_s.at[peer], seq_send.at[2, k], seq_recv.at[2, peer], seq=peer).wait_recv()

        misc[1:2] = jnp.max(top_s[...].reshape(ns, 128), axis=0, keepdims=True)

    def scatter_sum(left, weight, half_send, half_recv, part_send, part_recv, phase, early, late):
        def product(parity):
            picked = jnp.concatenate([left[2 * i + parity] for i in range(nx)], axis=0)
            return dot(picked, weight[...]).reshape(nx, rows, width)

        half_send[...] = product(1 - core).astype(BF16)
        over = remote(half_send, half_recv, rs_send.at[phase, 0], rs_recv.at[phase, nx], tensor=sibling)
        over.start()
        own_sum[...] = product(core)
        early()
        over.wait_recv()
        sent = [over]
        for k in range(1, nx):
            dest = (x + k) % nx
            part_send[k] = (own_sum[dest] + half_recv[dest].astype(F32)).astype(BF16)
            copy = remote(
                part_send.at[k], part_recv.at[x], rs_send.at[phase, k], rs_recv.at[phase, x], tensor=dest * 2 + core
            )
            copy.start()
            sent.append(copy)
        total = own_sum[x] + half_recv[x].astype(F32)
        late()
        for k in range(1, nx):
            source = (x + nx - k) % nx
            remote(
                part_send.at[k], part_recv.at[source], rs_send.at[phase, k], rs_recv.at[phase, source], tensor=sibling
            ).wait_recv()
            total = total + part_recv[source].astype(F32)
        for copy in sent:
            copy.wait_send()
        return total

    for i in range(3, 8):
        loads[i].wait()
    last_projected()
    summed = scatter_sum(attn, wo, half_send1, half_recv1, part_send1, part_recv1, 0, lambda: None, last_inner)
    mid = (hidden[...].astype(F32) + summed).astype(BF16).astype(F32)
    full2[me_t] = rms_scale(mid, ff_gain[...])
    copies = gather_start(full2, 1)
    last_final()
    all_rows = gather_finish(full2, 1, copies)
    last_logits()
    gate = dot(all_rows, wg[...])
    up = dot(all_rows, wu[...])
    inner = (jax.nn.gelu(gate, approximate=True) * up).astype(BF16)
    inner_rows[...] = inner.reshape(nt, rows, inner.shape[1])
    top_of_words()
    total = scatter_sum(inner_rows, wd, half_send2, half_recv2, part_send2, part_recv2, 1, top_of_group, lambda: None)
    result = (mid + total).astype(BF16)
    out[...] = result

    top_of_all()
    for send in sends:
        send.wait_send()

    @pl.loop(1, ns)
    def _(k):
        peer = seq_peer(k)
        remote(kv_in.at[peer], slots.at[me_s], seq_send.at[0, k], seq_recv.at[0, me_s], seq=peer).wait_send()
        remote(last_send.at[me_t], last_all.at[me_s], seq_send.at[1, k], seq_recv.at[1, me_s], seq=peer).wait_send()
        remote(top_s.at[me_s], top_s.at[me_s], seq_send.at[2, k], seq_recv.at[2, me_s], seq=peer).wait_send()

    @pl.loop(0, nz - 1)
    def _(i):
        over_z(i).wait_send()

    @pl.loop(0, nz)
    def _(column):
        for k in range(1, ny):
            for copy in over_y(k, column):
                copy.wait_send()


def per_device(
    hidden,
    attn_gain,
    attn_query,
    attn_key,
    attn_value,
    attn_out,
    ff_gain,
    ff_gate,
    ff_up,
    ff_down,
    final_gain,
    embedding,
    rel_weight,
    bucket_table,
    prefix_kv,
    node_lengths,
    group_branch,
    node_slot,
    request_group,
):
    ns = lax.axis_size("seq")
    nt = lax.axis_size("tensor")
    nx = nt // 2
    nz = 8 if ns % 8 == 0 else ns
    ny = ns // nz
    rows, width = hidden.shape
    suf = rows * nt
    heads = rel_weight.shape[1]
    cols = attn_query.shape[1]
    cap = prefix_kv.shape[2]
    chunk = 2 * cap // ns
    per = 128 * pl.cdiv(pl.cdiv(embedding.shape[0], nt), 128)
    kv_chunks = prefix_kv.reshape(ns, chunk, cols)
    smem = pl.BlockSpec(memory_space=pltpu.SMEM)
    vmem = pl.BlockSpec(memory_space=pltpu.VMEM)
    hbm = pl.BlockSpec(memory_space=pl.ANY)
    weights = (attn_query, attn_key, attn_value, attn_out, ff_gate, ff_up, ff_down, embedding)
    dma = pltpu.SemaphoreType.DMA
    result, misc = pl.pallas_call(
        functools.partial(kernel, ns, nt),
        out_shape=(jax.ShapeDtypeStruct((rows, width), BF16), jax.ShapeDtypeStruct((8, 128), F32)),
        in_specs=[smem] * 5 + [vmem] * 5 + [hbm] * 9,
        out_specs=(vmem, vmem),
        scratch_shapes=[pltpu.VMEM(w.shape, BF16) for w in weights]
        + [
            pltpu.VMEM((nt, rows, width), BF16),
            pltpu.VMEM((nt, rows, width), BF16),
            pltpu.VMEM((ns, chunk, cols), BF16),
            pltpu.VMEM((nz, 1 + 2 * ny, chunk, cols), BF16),
            pltpu.VMEM((nz, 1 + 2 * ny, chunk, cols), BF16),
            pltpu.VMEM((3, ns, chunk, cols), BF16),
            pltpu.VMEM((heads, 4, suf // 2, suf + suf // 2), F32),
            pltpu.VMEM((suf, cols), BF16),
            pltpu.VMEM((suf, cols), BF16),
            pltpu.VMEM((suf, cols), BF16),
            pltpu.VMEM((nt, rows, cols), BF16),
            pltpu.VMEM((nt, rows, ff_down.shape[0]), BF16),
        ]
        + [pltpu.VMEM((nx, rows, width), BF16) for _ in range(8)]
        + [
            pltpu.VMEM((nx, rows, width), F32),
            pltpu.VMEM((nt, 1, cols + 128), F32),
            pltpu.VMEM((2, 1, width), F32),
            pltpu.VMEM((2, nt, 1, width), F32),
            pltpu.VMEM((ns, 1, cols + 128), F32),
            pltpu.VMEM((nt, ns, per), F32),
            pltpu.VMEM((nt, ns, per), F32),
            pltpu.VMEM((nt, 1, 128), F32),
            pltpu.VMEM((ns, 1, 128), F32),
            dma((len(weights) + 1,)),
            dma((2, 2 * nx)),
            dma((2, nt)),
            dma((2, nx)),
            dma((2, nx + 1)),
            dma((3, ns)),
            dma((3, ns)),
            dma((nz - 1,)),
            dma((nz,)),
            dma((2, ny, nz)),
            dma((2, ns)),
            dma((4, nt)),
            dma((4, nt)),
        ],
        compiler_params=pltpu.CompilerParams(collective_id=0, has_side_effects=True, vmem_limit_bytes=60 << 20),
        name="layer",
    )(
        node_lengths,
        group_branch,
        node_slot,
        request_group,
        rel_weight.T,
        hidden,
        attn_gain.reshape(1, -1),
        ff_gain.reshape(1, -1),
        final_gain.reshape(1, -1),
        bucket_table.reshape(1, -1),
        kv_chunks,
        *weights,
    )
    return result, misc[0, :ns], misc[1, :ns]


def solution(mesh):
    return jax.shard_map(
        per_device,
        mesh=mesh,
        in_specs=(
            P(("seq", "tensor"), None),
            P(),
            P(None, "tensor"),
            P(None, "tensor"),
            P(None, "tensor"),
            P("tensor", None),
            P(),
            P(None, "tensor"),
            P(None, "tensor"),
            P("tensor", None),
            P(),
            P("seq", "tensor"),
            P(None, "tensor"),
            P(),
            P(None, "seq", None, "tensor"),
            P(),
            P(),
            P(),
            P(),
        ),
        out_specs=(P(("seq", "tensor"), None), P(), P()),
        check_vma=False,
    )
```

```python
import functools

import jax
import jax.numpy as jnp
from jax import lax
from jax.experimental import pallas as pl
from jax.experimental.pallas import tpu as pltpu
from jax.sharding import PartitionSpec as P

MESH = pl.DeviceIdType.MESH
BRANCHES = 7
EPS = 1e-06
MASKED = -1e30
F32 = jnp.float32
BF16 = jnp.bfloat16
NT = (((1,), (1,)), ((), ()))


def remote(src, dst, send_sem, recv_sem, **device):
    return pltpu.make_async_remote_copy(
        src_ref=src, dst_ref=dst, send_sem=send_sem, recv_sem=recv_sem, device_id=device, device_id_type=MESH
    )


def dot(a, b):
    return jnp.dot(a, b, preferred_element_type=F32)


def rms_scale(values, gain):
    mean_square = jnp.mean(values * values, axis=-1, keepdims=True)
    return (values * lax.rsqrt(mean_square + EPS) * gain).astype(BF16)


def kernel(
    ns,
    nt,
    node_lengths,
    group_branch,
    node_slot,
    request_group,
    rel_weight,
    hidden,
    attn_gain,
    ff_gain,
    final_gain,
    bucket_table,
    kv_in,
    wq_in,
    wk_in,
    wv_in,
    wo_in,
    wg_in,
    wu_in,
    wd_in,
    emb_in,
    out,
    misc,
    wq,
    wk,
    wv,
    wo,
    wg,
    wu,
    wd,
    emb,
    full1,
    full2,
    slots,
    kv_send,
    path_root,
    path_kv,
    bias,
    query,
    own_key,
    own_value,
    attn,
    inner_rows,
    half_send1,
    half_recv1,
    part_send1,
    part_recv1,
    half_send2,
    half_recv2,
    part_send2,
    part_recv2,
    own_sum,
    last_send,
    row_out,
    row_in,
    last_all,
    logit_send,
    logit_all,
    top_t,
    top_s,
    wsem,
    ag_send,
    ag_recv,
    rs_send,
    rs_recv,
    seq_send,
    seq_recv,
    z_send,
    z_recv,
    y_send,
    y_recv,
    tail_send,
    tail_recv,
):
    nx = nt // 2
    nz = 8 if ns % 8 == 0 else ns
    ny = ns // nz
    me_s = lax.axis_index("seq")
    me_t = lax.axis_index("tensor")
    x, core = me_t // 2, me_t % 2
    y, z = me_s // nz, me_s % nz
    sibling = me_t + 1 - 2 * core
    rows, width = hidden.shape
    suf = rows * nt
    heads, buckets = rel_weight.shape
    cols = wq.shape[1]
    chunk = kv_in.shape[1]
    cap = chunk * ns // 2

    def seq_peer(k):
        return ((y + k // nz) % ny) * nz + (z + k % nz) % nz

    def seq_from(k):
        return ((y + ny - k // nz) % ny) * nz + (z + nz - k % nz) % nz

    weights = [(wq_in, wq), (wk_in, wk), (wv_in, wv), (wo_in, wo), (wg_in, wg), (wu_in, wu), (wd_in, wd), (emb_in, emb)]
    loads = [pltpu.make_async_copy(a, b, wsem.at[i]) for i, (a, b) in enumerate(weights)]
    own_slot = pltpu.make_async_copy(kv_in.at[me_s], slots.at[me_s], wsem.at[len(weights)])
    own_slot.start()
    for load in loads:
        load.start()

    barrier = pltpu.get_barrier_semaphore()

    @pl.loop(1, ns)
    def _(k):
        pl.semaphore_signal(barrier, inc=1, device_id={"seq": seq_peer(k)}, device_id_type=MESH)

    for k in range(1, nt):
        pl.semaphore_signal(barrier, inc=1, device_id={"tensor": (me_t + k) % nt}, device_id_type=MESH)

    full1[me_t] = rms_scale(hidden[...].astype(F32), attn_gain[...])
    pl.semaphore_wait(barrier, ns - 1 + nt - 1)

    @pl.loop(1, ns)
    def _(k):
        peer = seq_peer(k)
        remote(kv_in.at[peer], slots.at[me_s], seq_send.at[0, k], seq_recv.at[0, me_s], seq=peer).start()

    def gather_start(buf, phase):
        copies = [remote(buf.at[me_t], buf.at[me_t], ag_send.at[phase, 0], ag_recv.at[phase, me_t], tensor=sibling)]
        for k in range(1, nx):
            peer = ((x + k) % nx) * 2 + core
            copies.append(remote(buf.at[me_t], buf.at[me_t], ag_send.at[phase, k], ag_recv.at[phase, me_t], tensor=peer))
        for copy in copies:
            copy.start()
        return copies

    def gather_finish(buf, phase, copies):
        for k in range(1, nx):
            block = ((x + nx - k) % nx) * 2 + core
            remote(buf.at[block], buf.at[block], ag_send.at[phase, nx], ag_recv.at[phase, block], tensor=sibling).wait_recv()
            copy = remote(
                buf.at[block], buf.at[block], ag_send.at[phase, nx - 1 + k], ag_recv.at[phase, block], tensor=sibling
            )
            copy.start()
            copies.append(copy)
        for k in range(nx):
            block = ((x + nx - k) % nx) * 2 + 1 - core
            remote(buf.at[block], buf.at[block], ag_send.at[phase, nx], ag_recv.at[phase, block], tensor=sibling).wait_recv()
        for copy in copies:
            copy.wait_send()
        return buf[...].reshape(suf, width)

    copies = gather_start(full1, 0)

    def path_of(request):
        group = request_group[request]
        return 0, 1 + group_branch[group], 1 + BRANCHES + group

    nodes = path_of(me_s)
    lengths = [node_lengths[n] for n in nodes]
    base = lengths[0] + lengths[1] + lengths[2]
    starts = [0, lengths[0], lengths[0] + lengths[1], base]

    rels = bucket_table.shape[1]
    table = jnp.broadcast_to(bucket_table[...], (8, rels))
    sub = lax.broadcasted_iota(jnp.int32, (8, 1), 0)
    head_bias = jnp.zeros((8, rels), F32)
    for b in range(buckets):
        column = jnp.zeros((8, 1), F32)
        for h in range(heads):
            column = jnp.where(sub == h, rel_weight[h, b], column)
        head_bias = jnp.where(table == b, column, head_bias)
    half = suf // 2
    span = 2 * suf
    for part in range(4):
        first = rels // 2 - suf + 1 + starts[part] - base
        slab = pltpu.roll(head_bias, rels - first, 1)[:, :span]
        for h in range(heads):
            spread = jnp.broadcast_to(slab[h : h + 1, :], (half, span))
            turned = pltpu.roll(spread, span - half + 1, 1, stride=1, stride_axis=0)
            bias[h, part] = turned[:, : span - half]

    @pl.loop(1, ns)
    def _(k):
        peer = seq_from(k)
        remote(kv_in.at[peer], slots.at[peer], seq_send.at[0, k], seq_recv.at[0, peer], seq=peer).wait_recv()

    own_slot.wait()

    path_root[me_s] = slots[node_slot[0]]

    def root_z(k):
        to = y * nz + (z + k) % nz
        return remote(path_root.at[me_s], path_root.at[me_s], z_send.at[k], z_recv.at[z], seq=to)

    def root_y(k):
        row = path_root.at[pl.ds(y * nz, nz)]
        return remote(row, row, y_send.at[k], y_recv.at[y], seq=((y + k) % ny) * nz + z)

    for k in range(1, nz):
        root_z(k).start()

    @pl.loop(1, ns)
    def _(k):
        peer = seq_peer(k)
        for level, node in enumerate(path_of(peer)[1:]):
            kv_send[k, level] = slots[node_slot[node]]
        remote(kv_send.at[k], path_kv.at[:, me_s], seq_send.at[1, k], seq_recv.at[1, me_s], seq=peer).start()

    for level, node in enumerate(nodes[1:]):
        path_kv[level, me_s] = slots[node_slot[node]]

    for k in range(1, nz):
        column = (z + nz - k) % nz
        at = y * nz + column
        remote(path_root.at[at], path_root.at[at], z_send.at[k], z_recv.at[column], seq=at).wait_recv()
    for k in range(1, ny):
        root_y(k).start()

    all_rows = gather_finish(full1, 0, copies)
    for i, (weight, result) in enumerate(((wq, query), (wk, own_key), (wv, own_value))):
        loads[i].wait()
        result[...] = dot(all_rows, weight[...]).astype(BF16)

    @pl.loop(1, ns)
    def _(k):
        peer = seq_from(k)
        remote(kv_send.at[k], path_kv.at[:, peer], seq_send.at[1, k], seq_recv.at[1, peer], seq=peer).wait_recv()

    for k in range(1, ny):
        row = (y + ny - k) % ny
        chunks = path_root.at[pl.ds(row * nz, nz)]
        remote(chunks, chunks, y_send.at[k], y_recv.at[row], seq=row * nz + z).wait_recv()

    lane = lax.broadcasted_iota(jnp.int32, (1, cap), 1)
    penalty = [jnp.where(lane < lengths[level], 0.0, MASKED) for level in range(3)]
    pair_lane = lax.broadcasted_iota(jnp.int32, (1, 128), 1)
    per_pair = 128 // (cols // heads)
    half_chunks = ns // 2
    for pair in range(cols // 128):
        at = slice(pair * 128, pair * 128 + 128)
        paths = (path_root, path_kv.at[0], path_kv.at[1])
        keys = [path[:half_chunks, :, at].reshape(cap, 128) for path in paths] + [own_key[:, at]]
        values = [path[half_chunks:, :, at].reshape(cap, 128) for path in paths] + [own_value[:, at]]
        for block in range(2):
            pair_query = query[block * half : block * half + half, at]
            merged = None
            for e in range(per_pair):
                h = pair * per_pair + e
                mine = pair_lane // (128 // per_pair) == e
                head_query = jnp.where(mine, pair_query, jnp.zeros((), BF16))
                scores = []
                for part in range(4):
                    score = lax.dot_general(head_query, keys[part], NT, preferred_element_type=F32)
                    score = score + bias[h, part, :, half * (1 - block) : half * (1 - block) + suf]
                    scores.append(score + penalty[part] if part < 3 else score)
                peak = jnp.max(jnp.maximum(jnp.maximum(scores[0], scores[1]), jnp.maximum(scores[2], scores[3])), axis=1, keepdims=True)
                total = None
                summed = None
                for part in range(4):
                    prob = jnp.exp(scores[part] - peak)
                    total = prob if total is None else total + prob
                    term = dot(prob.astype(BF16), values[part])
                    summed = term if summed is None else summed + term
                head_out = summed / jnp.sum(total, axis=1, keepdims=True)
                merged = head_out if merged is None else jnp.where(mine, head_out, merged)
            merged = merged.astype(BF16)
            for r in range(half // rows):
                attn[block * (half // rows) + r, :, at] = merged[r * rows : r * rows + rows]

    def row_send(row, phase):
        row_out[phase] = row
        for k in range(1, nt):
            peer = (me_t + k) % nt
            send = remote(
                row_out.at[phase], row_in.at[phase, me_t], tail_send.at[phase, k], tail_recv.at[phase, me_t], tensor=peer
            )
            send.start()
            sends.append(send)

    def row_sum(phase):
        row = row_out[phase]
        for k in range(1, nt):
            peer = (me_t + nt - k) % nt
            remote(
                row_out.at[phase], row_in.at[phase, peer], tail_send.at[phase, k], tail_recv.at[phase, peer], tensor=peer
            ).wait_recv()
            row = row + row_in[phase, peer]
        return row

    sends = []
    is_last = me_t == nt - 1

    def last_projected():
        row = dot(attn[nt - 1, rows - 16 : rows], wo[...])[15:16]
        row_send(row + jnp.where(is_last, hidden[rows - 1 : rows].astype(F32), 0.0), 0)

    def last_inner():
        row = row_sum(0).astype(BF16).astype(F32)
        left = jnp.broadcast_to(rms_scale(row, ff_gain[...]).astype(F32), (16, width)).astype(BF16)
        inner = (jax.nn.gelu(dot(left, wg[...]), approximate=True) * dot(left, wu[...])).astype(BF16)
        row_send(dot(inner, wd[...])[0:1] + jnp.where(is_last, row, 0.0), 1)

    def last_final():
        last = row_sum(1).astype(BF16).astype(F32)
        mean_square = jnp.mean(last * last, axis=-1, keepdims=True)
        rms = jnp.broadcast_to(jnp.sqrt(mean_square), (1, 128))
        final = (last * lax.rsqrt(mean_square + EPS) * final_gain[...]).astype(BF16).astype(F32)
        for t in range(nt):
            last_send[t] = jnp.concatenate([final[:, t * cols : t * cols + cols], rms], axis=1)

        @pl.loop(1, ns)
        def _(k):
            remote(
                last_send.at[me_t], last_all.at[me_s], seq_send.at[2, k], seq_recv.at[2, me_s], seq=seq_peer(k)
            ).start()

        last_all[me_s] = last_send[me_t]

    per = logit_send.shape[2]
    diagonal = lax.broadcasted_iota(jnp.int32, (ns, 128), 0) == lax.broadcasted_iota(jnp.int32, (ns, 128), 1)

    def last_logits():
        @pl.loop(1, ns)
        def _(k):
            peer = seq_from(k)
            remote(
                last_send.at[me_t], last_all.at[peer], seq_send.at[2, k], seq_recv.at[2, peer], seq=peer
            ).wait_recv()

        lasts = last_all[...].reshape(ns, cols + 128)
        vocab = emb.shape[0]
        logits = lax.dot_general(lasts[:, :cols].astype(BF16), emb[...], NT, preferred_element_type=F32)
        logits = jnp.concatenate([logits, jnp.full((ns, per * nt - vocab), MASKED, F32)], axis=1)
        for t in range(nt):
            logit_send[t] = logits[:, t * per : t * per + per]
        for k in range(1, nt):
            peer = (me_t + k) % nt
            send = remote(logit_send.at[peer], logit_all.at[me_t], tail_send.at[2, k], tail_recv.at[2, me_t], tensor=peer)
            send.start()
            sends.append(send)
        misc[0:1] = jnp.sum(jnp.where(diagonal, lasts[:, cols:], 0.0), axis=0, keepdims=True)

    def top_of_words():
        logit = logit_send[me_t]
        for k in range(1, nt):
            peer = (me_t + nt - k) % nt
            remote(
                logit_send.at[peer], logit_all.at[peer], tail_send.at[2, k], tail_recv.at[2, peer], tensor=peer
            ).wait_recv()
            logit = logit + logit_all[peer]
        highest = jnp.max(logit, axis=1, keepdims=True)
        top_t[me_t] = jnp.max(jnp.where(diagonal, highest, 2 * nt * MASKED), axis=0, keepdims=True)
        for k in range(1, nt):
            peer = (me_t + k) % nt
            send = remote(top_t.at[me_t], top_t.at[me_t], tail_send.at[3, k], tail_recv.at[3, me_t], tensor=peer)
            send.start()
            sends.append(send)

    def top_of_group():
        top = top_t[me_t]
        for k in range(1, nt):
            peer = (me_t + nt - k) % nt
            remote(top_t.at[peer], top_t.at[peer], tail_send.at[3, k], tail_recv.at[3, peer], tensor=peer).wait_recv()
            top = jnp.maximum(top, top_t[peer])
        top_s[me_s] = top

        @pl.loop(1, ns)
        def _(k):
            remote(top_s.at[me_s], top_s.at[me_s], seq_send.at[3, k], seq_recv.at[3, me_s], seq=seq_peer(k)).start()

    def top_of_all():
        @pl.loop(1, ns)
        def _(k):
            peer = seq_from(k)
            remote(top_s.at[peer], top_s.at[peer], seq_send.at[3, k], seq_recv.at[3, peer], seq=peer).wait_recv()

        misc[1:2] = jnp.max(top_s[...].reshape(ns, 128), axis=0, keepdims=True)

    def scatter_sum(left, weight, half_send, half_recv, part_send, part_recv, phase, early, late):
        def product(parity):
            picked = jnp.concatenate([left[2 * i + parity] for i in range(nx)], axis=0)
            return dot(picked, weight[...]).reshape(nx, rows, width)

        half_send[...] = product(1 - core).astype(BF16)
        over = remote(half_send, half_recv, rs_send.at[phase, 0], rs_recv.at[phase, nx], tensor=sibling)
        over.start()
        own_sum[...] = product(core)
        early()
        over.wait_recv()
        sent = [over]
        for k in range(1, nx):
            dest = (x + k) % nx
            part_send[k] = (own_sum[dest] + half_recv[dest].astype(F32)).astype(BF16)
            copy = remote(
                part_send.at[k], part_recv.at[x], rs_send.at[phase, k], rs_recv.at[phase, x], tensor=dest * 2 + core
            )
            copy.start()
            sent.append(copy)
        total = own_sum[x] + half_recv[x].astype(F32)
        late()
        for k in range(1, nx):
            source = (x + nx - k) % nx
            remote(
                part_send.at[k], part_recv.at[source], rs_send.at[phase, k], rs_recv.at[phase, source], tensor=sibling
            ).wait_recv()
            total = total + part_recv[source].astype(F32)
        for copy in sent:
            copy.wait_send()
        return total

    for i in range(3, 8):
        loads[i].wait()
    last_projected()
    summed = scatter_sum(attn, wo, half_send1, half_recv1, part_send1, part_recv1, 0, lambda: None, last_inner)
    mid = (hidden[...].astype(F32) + summed).astype(BF16).astype(F32)
    full2[me_t] = rms_scale(mid, ff_gain[...])
    copies = gather_start(full2, 1)
    last_final()
    all_rows = gather_finish(full2, 1, copies)
    last_logits()
    gate = dot(all_rows, wg[...])
    up = dot(all_rows, wu[...])
    inner = (jax.nn.gelu(gate, approximate=True) * up).astype(BF16)
    inner_rows[...] = inner.reshape(nt, rows, inner.shape[1])
    top_of_words()
    total = scatter_sum(inner_rows, wd, half_send2, half_recv2, part_send2, part_recv2, 1, top_of_group, lambda: None)
    result = (mid + total).astype(BF16)
    out[...] = result

    top_of_all()
    for send in sends:
        send.wait_send()

    @pl.loop(1, ns)
    def _(k):
        peer = seq_peer(k)
        remote(kv_in.at[peer], slots.at[me_s], seq_send.at[0, k], seq_recv.at[0, me_s], seq=peer).wait_send()
        remote(kv_send.at[k], path_kv.at[:, me_s], seq_send.at[1, k], seq_recv.at[1, me_s], seq=peer).wait_send()
        remote(last_send.at[me_t], last_all.at[me_s], seq_send.at[2, k], seq_recv.at[2, me_s], seq=peer).wait_send()
        remote(top_s.at[me_s], top_s.at[me_s], seq_send.at[3, k], seq_recv.at[3, me_s], seq=peer).wait_send()

    for k in range(1, nz):
        root_z(k).wait_send()
    for k in range(1, ny):
        root_y(k).wait_send()


def per_device(
    hidden,
    attn_gain,
    attn_query,
    attn_key,
    attn_value,
    attn_out,
    ff_gain,
    ff_gate,
    ff_up,
    ff_down,
    final_gain,
    embedding,
    rel_weight,
    bucket_table,
    prefix_kv,
    node_lengths,
    group_branch,
    node_slot,
    request_group,
):
    ns = lax.axis_size("seq")
    nt = lax.axis_size("tensor")
    nx = nt // 2
    nz = 8 if ns % 8 == 0 else ns
    ny = ns // nz
    rows, width = hidden.shape
    suf = rows * nt
    heads = rel_weight.shape[1]
    cols = attn_query.shape[1]
    cap = prefix_kv.shape[2]
    chunk = 2 * cap // ns
    per = 128 * pl.cdiv(pl.cdiv(embedding.shape[0], nt), 128)
    kv_chunks = prefix_kv.reshape(ns, chunk, cols)
    smem = pl.BlockSpec(memory_space=pltpu.SMEM)
    vmem = pl.BlockSpec(memory_space=pltpu.VMEM)
    hbm = pl.BlockSpec(memory_space=pl.ANY)
    weights = (attn_query, attn_key, attn_value, attn_out, ff_gate, ff_up, ff_down, embedding)
    dma = pltpu.SemaphoreType.DMA
    result, misc = pl.pallas_call(
        functools.partial(kernel, ns, nt),
        out_shape=(jax.ShapeDtypeStruct((rows, width), BF16), jax.ShapeDtypeStruct((8, 128), F32)),
        in_specs=[smem] * 5 + [vmem] * 5 + [hbm] * 9,
        out_specs=(vmem, vmem),
        scratch_shapes=[pltpu.VMEM(w.shape, BF16) for w in weights]
        + [
            pltpu.VMEM((nt, rows, width), BF16),
            pltpu.VMEM((nt, rows, width), BF16),
            pltpu.VMEM((ns, chunk, cols), BF16),
            pltpu.VMEM((ns, 2, chunk, cols), BF16),
            pltpu.VMEM((ns, chunk, cols), BF16),
            pltpu.VMEM((2, ns, chunk, cols), BF16),
            pltpu.VMEM((heads, 4, suf // 2, suf + suf // 2), F32),
            pltpu.VMEM((suf, cols), BF16),
            pltpu.VMEM((suf, cols), BF16),
            pltpu.VMEM((suf, cols), BF16),
            pltpu.VMEM((nt, rows, cols), BF16),
            pltpu.VMEM((nt, rows, ff_down.shape[0]), BF16),
        ]
        + [pltpu.VMEM((nx, rows, width), BF16) for _ in range(8)]
        + [
            pltpu.VMEM((nx, rows, width), F32),
            pltpu.VMEM((nt, 1, cols + 128), F32),
            pltpu.VMEM((2, 1, width), F32),
            pltpu.VMEM((2, nt, 1, width), F32),
            pltpu.VMEM((ns, 1, cols + 128), F32),
            pltpu.VMEM((nt, ns, per), F32),
            pltpu.VMEM((nt, ns, per), F32),
            pltpu.VMEM((nt, 1, 128), F32),
            pltpu.VMEM((ns, 1, 128), F32),
            dma((len(weights) + 1,)),
            dma((2, 2 * nx)),
            dma((2, nt)),
            dma((2, nx)),
            dma((2, nx + 1)),
            dma((4, ns)),
            dma((4, ns)),
            dma((nz,)),
            dma((nz,)),
            dma((ny,)),
            dma((ny,)),
            dma((4, nt)),
            dma((4, nt)),
        ],
        compiler_params=pltpu.CompilerParams(collective_id=0, has_side_effects=True, vmem_limit_bytes=60 << 20),
        name="layer",
    )(
        node_lengths,
        group_branch,
        node_slot,
        request_group,
        rel_weight.T,
        hidden,
        attn_gain.reshape(1, -1),
        ff_gain.reshape(1, -1),
        final_gain.reshape(1, -1),
        bucket_table.reshape(1, -1),
        kv_chunks,
        *weights,
    )
    return result, misc[0, :ns], misc[1, :ns]


def solution(mesh):
    return jax.shard_map(
        per_device,
        mesh=mesh,
        in_specs=(
            P(("seq", "tensor"), None),
            P(),
            P(None, "tensor"),
            P(None, "tensor"),
            P(None, "tensor"),
            P("tensor", None),
            P(),
            P(None, "tensor"),
            P(None, "tensor"),
            P("tensor", None),
            P(),
            P("seq", "tensor"),
            P(None, "tensor"),
            P(),
            P(None, "seq", None, "tensor"),
            P(),
            P(),
            P(),
            P(),
        ),
        out_specs=(P(("seq", "tensor"), None), P(), P()),
        check_vma=False,
    )
```

```python
import functools

import jax
import jax.numpy as jnp
from jax import lax
from jax.experimental import pallas as pl
from jax.experimental.pallas import tpu as pltpu
from jax.sharding import PartitionSpec as P

MESH = pl.DeviceIdType.MESH
BRANCHES = 7
EPS = 1e-06
MASKED = -1e30
F32 = jnp.float32
BF16 = jnp.bfloat16
NT = (((1,), (1,)), ((), ()))


def remote(src, dst, send_sem, recv_sem, **device):
    return pltpu.make_async_remote_copy(
        src_ref=src, dst_ref=dst, send_sem=send_sem, recv_sem=recv_sem, device_id=device, device_id_type=MESH
    )


def dot(a, b):
    return jnp.dot(a, b, preferred_element_type=F32)


def rms_scale(values, gain):
    mean_square = jnp.mean(values * values, axis=-1, keepdims=True)
    return (values * lax.rsqrt(mean_square + EPS) * gain).astype(BF16)


def kernel(
    ns,
    nt,
    node_lengths,
    group_branch,
    node_slot,
    request_group,
    rel_weight,
    hidden,
    attn_gain,
    ff_gain,
    final_gain,
    bucket_table,
    kv_in,
    wq_in,
    wk_in,
    wv_in,
    wo_in,
    wg_in,
    wu_in,
    wd_in,
    emb_in,
    out,
    misc,
    wq,
    wk,
    wv,
    wo,
    wg,
    wu,
    wd,
    emb,
    full1,
    full2,
    slots,
    kv_send,
    path_root,
    path_kv,
    bias,
    query,
    own_key,
    own_value,
    attn,
    inner_rows,
    half_send,
    half_recv,
    part_send,
    part_recv,
    own_sum,
    mids,
    last_send,
    row_out,
    row_in,
    last_all,
    logit_send,
    logit_all,
    top_t,
    top_s,
    wsem,
    ag_send,
    ag_recv,
    rs_send,
    rs_recv,
    seq_send,
    seq_recv,
    z_send,
    z_recv,
    y_send,
    y_recv,
    tail_send,
    tail_recv,
):
    nx = nt // 2
    nz = 8 if ns % 8 == 0 else ns
    ny = ns // nz
    me_s = lax.axis_index("seq")
    me_t = lax.axis_index("tensor")
    x, core = me_t // 2, me_t % 2
    y, z = me_s // nz, me_s % nz
    sibling = me_t + 1 - 2 * core
    rows, width = hidden.shape
    suf = rows * nt
    heads, buckets = rel_weight.shape
    cols = wq.shape[1]
    chunk = kv_in.shape[1]
    cap = chunk * ns // 2

    def seq_peer(k):
        return ((y + k // nz) % ny) * nz + (z + k % nz) % nz

    def seq_from(k):
        return ((y + ny - k // nz) % ny) * nz + (z + nz - k % nz) % nz

    weights = [(wq_in, wq), (wk_in, wk), (wv_in, wv), (wo_in, wo), (wg_in, wg), (wu_in, wu), (wd_in, wd), (emb_in, emb)]
    loads = [pltpu.make_async_copy(a, b, wsem.at[i]) for i, (a, b) in enumerate(weights)]
    own_slot = pltpu.make_async_copy(kv_in.at[me_s], slots.at[me_s], wsem.at[len(weights)])
    own_slot.start()
    for load in loads:
        load.start()

    barrier = pltpu.get_barrier_semaphore()

    @pl.loop(1, ns)
    def _(k):
        pl.semaphore_signal(barrier, inc=1, device_id={"seq": seq_peer(k)}, device_id_type=MESH)

    for k in range(1, nt):
        pl.semaphore_signal(barrier, inc=1, device_id={"tensor": (me_t + k) % nt}, device_id_type=MESH)

    full1[me_t] = rms_scale(hidden[...].astype(F32), attn_gain[...])
    pl.semaphore_wait(barrier, ns - 1 + nt - 1)

    @pl.loop(1, ns)
    def _(k):
        peer = seq_peer(k)
        remote(kv_in.at[peer], slots.at[me_s], seq_send.at[0, k], seq_recv.at[0, me_s], seq=peer).start()

    def gather_start(buf, phase):
        copies = [remote(buf.at[me_t], buf.at[me_t], ag_send.at[phase, 0], ag_recv.at[phase, me_t], tensor=sibling)]
        for k in range(1, nx):
            peer = ((x + k) % nx) * 2 + core
            copies.append(remote(buf.at[me_t], buf.at[me_t], ag_send.at[phase, k], ag_recv.at[phase, me_t], tensor=peer))
        for copy in copies:
            copy.start()
        return copies

    def gather_finish(buf, phase, copies):
        for k in range(1, nx):
            block = ((x + nx - k) % nx) * 2 + core
            remote(buf.at[block], buf.at[block], ag_send.at[phase, nx], ag_recv.at[phase, block], tensor=sibling).wait_recv()
            copy = remote(
                buf.at[block], buf.at[block], ag_send.at[phase, nx - 1 + k], ag_recv.at[phase, block], tensor=sibling
            )
            copy.start()
            copies.append(copy)
        for k in range(nx):
            block = ((x + nx - k) % nx) * 2 + 1 - core
            remote(buf.at[block], buf.at[block], ag_send.at[phase, nx], ag_recv.at[phase, block], tensor=sibling).wait_recv()
        for copy in copies:
            copy.wait_send()
        return buf[...].reshape(nt * buf.shape[1], width)

    copies = gather_start(full1, 0)

    def path_of(request):
        group = request_group[request]
        return 0, 1 + group_branch[group], 1 + BRANCHES + group

    nodes = path_of(me_s)
    lengths = [node_lengths[n] for n in nodes]
    base = lengths[0] + lengths[1] + lengths[2]
    starts = [0, lengths[0], lengths[0] + lengths[1], base]

    rels = bucket_table.shape[1]
    table = jnp.broadcast_to(bucket_table[...], (8, rels))
    sub = lax.broadcasted_iota(jnp.int32, (8, 1), 0)
    head_bias = jnp.zeros((8, rels), F32)
    for b in range(buckets):
        column = jnp.zeros((8, 1), F32)
        for h in range(heads):
            column = jnp.where(sub == h, rel_weight[h, b], column)
        head_bias = jnp.where(table == b, column, head_bias)
    half = suf // 2
    span = 2 * suf
    for part in range(4):
        first = rels // 2 - suf + 1 + starts[part] - base
        slab = pltpu.roll(head_bias, rels - first, 1)[:, :span]
        for h in range(heads):
            spread = jnp.broadcast_to(slab[h : h + 1, :], (half, span))
            turned = pltpu.roll(spread, span - half + 1, 1, stride=1, stride_axis=0)
            bias[h, part] = turned[:, : span - half]

    @pl.loop(1, ns)
    def _(k):
        peer = seq_from(k)
        remote(kv_in.at[peer], slots.at[peer], seq_send.at[0, k], seq_recv.at[0, peer], seq=peer).wait_recv()

    own_slot.wait()

    path_root[me_s] = slots[node_slot[0]]

    def root_z(k):
        to = y * nz + (z + k) % nz
        return remote(path_root.at[me_s], path_root.at[me_s], z_send.at[k], z_recv.at[z], seq=to)

    def root_y(k):
        row = path_root.at[pl.ds(y * nz, nz)]
        return remote(row, row, y_send.at[k], y_recv.at[y], seq=((y + k) % ny) * nz + z)

    for k in range(1, nz):
        root_z(k).start()

    @pl.loop(1, ns)
    def _(k):
        peer = seq_peer(k)
        for level, node in enumerate(path_of(peer)[1:]):
            kv_send[k, level] = slots[node_slot[node]]
        remote(kv_send.at[k], path_kv.at[:, me_s], seq_send.at[1, k], seq_recv.at[1, me_s], seq=peer).start()

    for level, node in enumerate(nodes[1:]):
        path_kv[level, me_s] = slots[node_slot[node]]

    for k in range(1, nz):
        column = (z + nz - k) % nz
        at = y * nz + column
        remote(path_root.at[at], path_root.at[at], z_send.at[k], z_recv.at[column], seq=at).wait_recv()
    for k in range(1, ny):
        root_y(k).start()

    all_rows = gather_finish(full1, 0, copies)
    for i, (weight, result) in enumerate(((wq, query), (wk, own_key), (wv, own_value))):
        loads[i].wait()
        result[...] = dot(all_rows, weight[...]).astype(BF16)

    @pl.loop(1, ns)
    def _(k):
        peer = seq_from(k)
        remote(kv_send.at[k], path_kv.at[:, peer], seq_send.at[1, k], seq_recv.at[1, peer], seq=peer).wait_recv()

    for k in range(1, ny):
        row = (y + ny - k) % ny
        chunks = path_root.at[pl.ds(row * nz, nz)]
        remote(chunks, chunks, y_send.at[k], y_recv.at[row], seq=row * nz + z).wait_recv()

    lane = lax.broadcasted_iota(jnp.int32, (1, cap), 1)
    penalty = [jnp.where(lane < lengths[level], 0.0, MASKED) for level in range(3)]
    pair_lane = lax.broadcasted_iota(jnp.int32, (1, 128), 1)
    per_pair = 128 // (cols // heads)
    half_chunks = ns // 2
    block_rows = rows // 2

    def attend(part_of):
        firsts = [t * rows + part_of * block_rows for t in range(nt)]
        for pair in range(cols // 128):
            at = slice(pair * 128, pair * 128 + 128)
            paths = (path_root, path_kv.at[0], path_kv.at[1])
            keys = [path[:half_chunks, :, at].reshape(cap, 128) for path in paths] + [own_key[:, at]]
            values = [path[half_chunks:, :, at].reshape(cap, 128) for path in paths] + [own_value[:, at]]
            pair_query = jnp.concatenate([query[f : f + block_rows, at] for f in firsts], axis=0)
            merged = None
            for e in range(per_pair):
                h = pair * per_pair + e
                mine = pair_lane // (128 // per_pair) == e
                head_query = jnp.where(mine, pair_query, jnp.zeros((), BF16))
                scores = []
                for part in range(4):
                    score = lax.dot_general(head_query, keys[part], NT, preferred_element_type=F32)
                    turned = [
                        bias[h, part, f % half : f % half + block_rows, pl.ds(half * (1 - f // half), suf)] for f in firsts
                    ]
                    score = score + jnp.concatenate(turned, axis=0)
                    scores.append(score + penalty[part] if part < 3 else score)
                highest = jnp.maximum(jnp.maximum(scores[0], scores[1]), jnp.maximum(scores[2], scores[3]))
                peak = jnp.max(highest, axis=1, keepdims=True)
                total = None
                summed = None
                for part in range(4):
                    prob = jnp.exp(scores[part] - peak)
                    total = prob if total is None else total + prob
                    term = dot(prob.astype(BF16), values[part])
                    summed = term if summed is None else summed + term
                head_out = summed / jnp.sum(total, axis=1, keepdims=True)
                merged = head_out if merged is None else jnp.where(mine, head_out, merged)
            attn[part_of, :, :, at] = merged.astype(BF16).reshape(nt, block_rows, 128)

    def row_send(row, phase):
        row_out[phase] = row
        for k in range(1, nt):
            peer = (me_t + k) % nt
            send = remote(
                row_out.at[phase], row_in.at[phase, me_t], tail_send.at[phase, k], tail_recv.at[phase, me_t], tensor=peer
            )
            send.start()
            sends.append(send)

    def row_sum(phase):
        row = row_out[phase]
        for k in range(1, nt):
            peer = (me_t + nt - k) % nt
            remote(
                row_out.at[phase], row_in.at[phase, peer], tail_send.at[phase, k], tail_recv.at[phase, peer], tensor=peer
            ).wait_recv()
            row = row + row_in[phase, peer]
        return row

    sends = []
    is_last = me_t == nt - 1

    def last_projected():
        row = dot(attn[1, nt - 1], wo[...])[block_rows - 1 : block_rows]
        row_send(row + jnp.where(is_last, hidden[rows - 1 : rows].astype(F32), 0.0), 0)

    def last_inner():
        row = row_sum(0).astype(BF16).astype(F32)
        left = jnp.broadcast_to(rms_scale(row, ff_gain[...]).astype(F32), (16, width)).astype(BF16)
        inner = (jax.nn.gelu(dot(left, wg[...]), approximate=True) * dot(left, wu[...])).astype(BF16)
        row_send(dot(inner, wd[...])[0:1] + jnp.where(is_last, row, 0.0), 1)

    def last_final():
        last = row_sum(1).astype(BF16).astype(F32)
        mean_square = jnp.mean(last * last, axis=-1, keepdims=True)
        rms = jnp.broadcast_to(jnp.sqrt(mean_square), (1, 128))
        final = (last * lax.rsqrt(mean_square + EPS) * final_gain[...]).astype(BF16).astype(F32)
        for t in range(nt):
            last_send[t] = jnp.concatenate([final[:, t * cols : t * cols + cols], rms], axis=1)

        @pl.loop(1, ns)
        def _(k):
            remote(
                last_send.at[me_t], last_all.at[me_s], seq_send.at[2, k], seq_recv.at[2, me_s], seq=seq_peer(k)
            ).start()

        last_all[me_s] = last_send[me_t]

    per = logit_send.shape[2]
    diagonal = lax.broadcasted_iota(jnp.int32, (ns, 128), 0) == lax.broadcasted_iota(jnp.int32, (ns, 128), 1)

    def last_logits():
        @pl.loop(1, ns)
        def _(k):
            peer = seq_from(k)
            remote(
                last_send.at[me_t], last_all.at[peer], seq_send.at[2, k], seq_recv.at[2, peer], seq=peer
            ).wait_recv()

        lasts = last_all[...].reshape(ns, cols + 128)
        vocab = emb.shape[0]
        logits = lax.dot_general(lasts[:, :cols].astype(BF16), emb[...], NT, preferred_element_type=F32)
        logits = jnp.concatenate([logits, jnp.full((ns, per * nt - vocab), MASKED, F32)], axis=1)
        for t in range(nt):
            logit_send[t] = logits[:, t * per : t * per + per]
        for k in range(1, nt):
            peer = (me_t + k) % nt
            send = remote(logit_send.at[peer], logit_all.at[me_t], tail_send.at[2, k], tail_recv.at[2, me_t], tensor=peer)
            send.start()
            sends.append(send)
        misc[0:1] = jnp.sum(jnp.where(diagonal, lasts[:, cols:], 0.0), axis=0, keepdims=True)

    def top_of_words():
        logit = logit_send[me_t]
        for k in range(1, nt):
            peer = (me_t + nt - k) % nt
            remote(
                logit_send.at[peer], logit_all.at[peer], tail_send.at[2, k], tail_recv.at[2, peer], tensor=peer
            ).wait_recv()
            logit = logit + logit_all[peer]
        highest = jnp.max(logit, axis=1, keepdims=True)
        top_t[me_t] = jnp.max(jnp.where(diagonal, highest, 2 * nt * MASKED), axis=0, keepdims=True)
        for k in range(1, nt):
            peer = (me_t + k) % nt
            send = remote(top_t.at[me_t], top_t.at[me_t], tail_send.at[3, k], tail_recv.at[3, me_t], tensor=peer)
            send.start()
            sends.append(send)

    def top_of_group():
        top = top_t[me_t]
        for k in range(1, nt):
            peer = (me_t + nt - k) % nt
            remote(top_t.at[peer], top_t.at[peer], tail_send.at[3, k], tail_recv.at[3, peer], tensor=peer).wait_recv()
            top = jnp.maximum(top, top_t[peer])
        top_s[me_s] = top

        @pl.loop(1, ns)
        def _(k):
            remote(top_s.at[me_s], top_s.at[me_s], seq_send.at[3, k], seq_recv.at[3, me_s], seq=seq_peer(k)).start()

    def top_of_all():
        @pl.loop(1, ns)
        def _(k):
            peer = seq_from(k)
            remote(top_s.at[peer], top_s.at[peer], seq_send.at[3, k], seq_recv.at[3, peer], seq=peer).wait_recv()

        misc[1:2] = jnp.max(top_s[...].reshape(ns, 128), axis=0, keepdims=True)

    def sum_begin(left, weight, i):
        def product(parity):
            picked = jnp.concatenate([left[2 * k + parity] for k in range(nx)], axis=0)
            return dot(picked, weight[...]).reshape(nx, block_rows, width)

        half_send[i] = product(1 - core).astype(BF16)
        over = remote(half_send.at[i], half_recv.at[i], rs_send.at[i, 0], rs_recv.at[i, nx], tensor=sibling)
        over.start()
        sends.append(over)
        own_sum[i] = product(core)

    others = [2, 1, 3] if nx == 4 else list(range(1, nx))

    def sum_parts(i):
        remote(half_send.at[i], half_recv.at[i], rs_send.at[i, 0], rs_recv.at[i, nx], tensor=sibling).wait_recv()
        for k in others:
            dest = (x + k) % nx
            part_send[i, k] = (own_sum[i, dest] + half_recv[i, dest].astype(F32)).astype(BF16)
            copy = remote(
                part_send.at[i, k], part_recv.at[i, x], rs_send.at[i, k], rs_recv.at[i, x], tensor=dest * 2 + core
            )
            copy.start()
            sends.append(copy)

    def sum_end(i):
        total = own_sum[i, x] + half_recv[i, x].astype(F32)
        for k in others:
            source = (x + nx - k) % nx
            remote(
                part_send.at[i, k], part_recv.at[i, source], rs_send.at[i, k], rs_recv.at[i, source], tensor=sibling
            ).wait_recv()
            total = total + part_recv[i, source].astype(F32)
        return total

    def own_rows(part_of):
        return pl.ds(part_of * block_rows, block_rows)

    def middle(part_of):
        total = sum_end(part_of)
        mid = (hidden[own_rows(part_of)].astype(F32) + total).astype(BF16)
        mids[part_of] = mid
        full2[part_of, me_t] = rms_scale(mid.astype(F32), ff_gain[...])
        return gather_start(full2.at[part_of], 1 + part_of)

    def feed_forward(all_rows, part_of):
        gate = dot(all_rows, wg[...])
        up = dot(all_rows, wu[...])
        inner = (jax.nn.gelu(gate, approximate=True) * up).astype(BF16)
        inner_rows[part_of] = inner.reshape(nt, block_rows, inner.shape[1])

    def finish(part_of):
        out[own_rows(part_of)] = (mids[part_of].astype(F32) + sum_end(2 + part_of)).astype(BF16)

    attend(1)
    for i in range(3, 8):
        loads[i].wait()
    last_projected()
    sum_begin(attn.at[1], wo, 1)
    attend(0)
    sum_parts(1)
    sum_begin(attn.at[0], wo, 0)
    last_inner()
    sum_parts(0)
    copies1 = middle(1)
    last_final()
    copies0 = middle(0)
    feed_forward(gather_finish(full2.at[1], 2, copies1), 1)
    sum_begin(inner_rows.at[1], wd, 3)
    last_logits()
    all_rows = gather_finish(full2.at[0], 1, copies0)
    sum_parts(3)
    feed_forward(all_rows, 0)
    top_of_words()
    sum_begin(inner_rows.at[0], wd, 2)
    sum_parts(2)
    top_of_group()
    finish(1)
    finish(0)

    top_of_all()
    for send in sends:
        send.wait_send()

    @pl.loop(1, ns)
    def _(k):
        peer = seq_peer(k)
        remote(kv_in.at[peer], slots.at[me_s], seq_send.at[0, k], seq_recv.at[0, me_s], seq=peer).wait_send()
        remote(kv_send.at[k], path_kv.at[:, me_s], seq_send.at[1, k], seq_recv.at[1, me_s], seq=peer).wait_send()
        remote(last_send.at[me_t], last_all.at[me_s], seq_send.at[2, k], seq_recv.at[2, me_s], seq=peer).wait_send()
        remote(top_s.at[me_s], top_s.at[me_s], seq_send.at[3, k], seq_recv.at[3, me_s], seq=peer).wait_send()

    for k in range(1, nz):
        root_z(k).wait_send()
    for k in range(1, ny):
        root_y(k).wait_send()


def per_device(
    hidden,
    attn_gain,
    attn_query,
    attn_key,
    attn_value,
    attn_out,
    ff_gain,
    ff_gate,
    ff_up,
    ff_down,
    final_gain,
    embedding,
    rel_weight,
    bucket_table,
    prefix_kv,
    node_lengths,
    group_branch,
    node_slot,
    request_group,
):
    ns = lax.axis_size("seq")
    nt = lax.axis_size("tensor")
    nx = nt // 2
    nz = 8 if ns % 8 == 0 else ns
    ny = ns // nz
    rows, width = hidden.shape
    suf = rows * nt
    heads = rel_weight.shape[1]
    cols = attn_query.shape[1]
    cap = prefix_kv.shape[2]
    chunk = 2 * cap // ns
    per = 128 * pl.cdiv(pl.cdiv(embedding.shape[0], nt), 128)
    kv_chunks = prefix_kv.reshape(ns, chunk, cols)
    smem = pl.BlockSpec(memory_space=pltpu.SMEM)
    vmem = pl.BlockSpec(memory_space=pltpu.VMEM)
    hbm = pl.BlockSpec(memory_space=pl.ANY)
    weights = (attn_query, attn_key, attn_value, attn_out, ff_gate, ff_up, ff_down, embedding)
    dma = pltpu.SemaphoreType.DMA
    result, misc = pl.pallas_call(
        functools.partial(kernel, ns, nt),
        out_shape=(jax.ShapeDtypeStruct((rows, width), BF16), jax.ShapeDtypeStruct((8, 128), F32)),
        in_specs=[smem] * 5 + [vmem] * 5 + [hbm] * 9,
        out_specs=(vmem, vmem),
        scratch_shapes=[pltpu.VMEM(w.shape, BF16) for w in weights]
        + [
            pltpu.VMEM((nt, rows, width), BF16),
            pltpu.VMEM((2, nt, rows // 2, width), BF16),
            pltpu.VMEM((ns, chunk, cols), BF16),
            pltpu.VMEM((ns, 2, chunk, cols), BF16),
            pltpu.VMEM((ns, chunk, cols), BF16),
            pltpu.VMEM((2, ns, chunk, cols), BF16),
            pltpu.VMEM((heads, 4, suf // 2, suf + suf // 2), F32),
            pltpu.VMEM((suf, cols), BF16),
            pltpu.VMEM((suf, cols), BF16),
            pltpu.VMEM((suf, cols), BF16),
            pltpu.VMEM((2, nt, rows // 2, cols), BF16),
            pltpu.VMEM((2, nt, rows // 2, ff_down.shape[0]), BF16),
        ]
        + [pltpu.VMEM((4, nx, rows // 2, width), BF16) for _ in range(4)]
        + [
            pltpu.VMEM((4, nx, rows // 2, width), F32),
            pltpu.VMEM((2, rows // 2, width), BF16),
            pltpu.VMEM((nt, 1, cols + 128), F32),
            pltpu.VMEM((2, 1, width), F32),
            pltpu.VMEM((2, nt, 1, width), F32),
            pltpu.VMEM((ns, 1, cols + 128), F32),
            pltpu.VMEM((nt, ns, per), F32),
            pltpu.VMEM((nt, ns, per), F32),
            pltpu.VMEM((nt, 1, 128), F32),
            pltpu.VMEM((ns, 1, 128), F32),
            dma((len(weights) + 1,)),
            dma((3, 2 * nx)),
            dma((3, nt)),
            dma((4, nx)),
            dma((4, nx + 1)),
            dma((4, ns)),
            dma((4, ns)),
            dma((nz,)),
            dma((nz,)),
            dma((ny,)),
            dma((ny,)),
            dma((4, nt)),
            dma((4, nt)),
        ],
        compiler_params=pltpu.CompilerParams(collective_id=0, has_side_effects=True, vmem_limit_bytes=60 << 20),
        name="layer",
    )(
        node_lengths,
        group_branch,
        node_slot,
        request_group,
        rel_weight.T,
        hidden,
        attn_gain.reshape(1, -1),
        ff_gain.reshape(1, -1),
        final_gain.reshape(1, -1),
        bucket_table.reshape(1, -1),
        kv_chunks,
        *weights,
    )
    return result, misc[0, :ns], misc[1, :ns]


def solution(mesh):
    return jax.shard_map(
        per_device,
        mesh=mesh,
        in_specs=(
            P(("seq", "tensor"), None),
            P(),
            P(None, "tensor"),
            P(None, "tensor"),
            P(None, "tensor"),
            P("tensor", None),
            P(),
            P(None, "tensor"),
            P(None, "tensor"),
            P("tensor", None),
            P(),
            P("seq", "tensor"),
            P(None, "tensor"),
            P(),
            P(None, "seq", None, "tensor"),
            P(),
            P(),
            P(),
            P(),
        ),
        out_specs=(P(("seq", "tensor"), None), P(), P()),
        check_vma=False,
    )
```

```python
import functools

import jax
import jax.numpy as jnp
from jax import lax
from jax.experimental import pallas as pl
from jax.experimental.pallas import tpu as pltpu
from jax.sharding import PartitionSpec as P

MESH = pl.DeviceIdType.MESH
BRANCHES = 7
EPS = 1e-06
MASKED = -1e30
F32 = jnp.float32
BF16 = jnp.bfloat16
NT = (((1,), (1,)), ((), ()))


def remote(src, dst, send_sem, recv_sem, **device):
    return pltpu.make_async_remote_copy(
        src_ref=src, dst_ref=dst, send_sem=send_sem, recv_sem=recv_sem, device_id=device, device_id_type=MESH
    )


def dot(a, b):
    return jnp.dot(a, b, preferred_element_type=F32)


def rms_scale(values, gain):
    mean_square = jnp.mean(values * values, axis=-1, keepdims=True)
    return (values * lax.rsqrt(mean_square + EPS) * gain).astype(BF16)


def kernel(
    ns,
    nt,
    node_lengths,
    group_branch,
    node_slot,
    request_group,
    rel_weight,
    hidden,
    attn_gain,
    ff_gain,
    final_gain,
    bucket_table,
    kv_in,
    wq_in,
    wk_in,
    wv_in,
    wo_in,
    wg_in,
    wu_in,
    wd_in,
    emb_in,
    out,
    misc,
    wq,
    wk,
    wv,
    wo,
    wg,
    wu,
    wd,
    emb,
    full1,
    full2,
    slots,
    kv_send,
    path_root,
    path_kv,
    bias,
    query,
    own_key,
    own_value,
    attn,
    inner_rows,
    half_send,
    half_recv,
    part_send,
    part_recv,
    own_sum,
    mids,
    last_send,
    row_out,
    row_in,
    last_all,
    logit_send,
    logit_all,
    top_t,
    top_s,
    wsem,
    ag_send,
    ag_recv,
    rs_send,
    rs_recv,
    seq_send,
    seq_recv,
    z_send,
    z_recv,
    y_send,
    y_recv,
    tail_send,
    tail_recv,
):
    nx = nt // 2
    nz = 8 if ns % 8 == 0 else ns
    ny = ns // nz
    me_s = lax.axis_index("seq")
    me_t = lax.axis_index("tensor")
    x, core = me_t // 2, me_t % 2
    y, z = me_s // nz, me_s % nz
    sibling = me_t + 1 - 2 * core
    rows, width = hidden.shape
    suf = rows * nt
    heads, buckets = rel_weight.shape
    cols = wq.shape[1]
    chunk = kv_in.shape[1]
    cap = chunk * ns // 2

    sends = []

    def seq_peer(k):
        return ((y + k // nz) % ny) * nz + (z + k % nz) % nz

    def seq_from(k):
        return ((y + ny - k // nz) % ny) * nz + (z + nz - k % nz) % nz

    weights = [(wq_in, wq), (wk_in, wk), (wv_in, wv), (wo_in, wo), (wg_in, wg), (wu_in, wu), (wd_in, wd), (emb_in, emb)]
    loads = [pltpu.make_async_copy(a, b, wsem.at[i]) for i, (a, b) in enumerate(weights)]
    own_slot = pltpu.make_async_copy(kv_in.at[me_s], slots.at[me_s], wsem.at[len(weights)])
    own_slot.start()
    for load in loads:
        load.start()

    barrier = pltpu.get_barrier_semaphore()

    @pl.loop(1, ns)
    def _(k):
        pl.semaphore_signal(barrier, inc=1, device_id={"seq": seq_peer(k)}, device_id_type=MESH)

    for k in range(1, nt):
        pl.semaphore_signal(barrier, inc=1, device_id={"tensor": (me_t + k) % nt}, device_id_type=MESH)

    full1[me_t] = rms_scale(hidden[...].astype(F32), attn_gain[...])
    pl.semaphore_wait(barrier, ns - 1 + nt - 1)

    @pl.loop(1, ns)
    def _(k):
        peer = seq_peer(k)
        remote(kv_in.at[peer], slots.at[me_s], seq_send.at[0, k], seq_recv.at[0, me_s], seq=peer).start()

    def gather_start(buf, phase):
        copies = [remote(buf.at[me_t], buf.at[me_t], ag_send.at[phase, 0], ag_recv.at[phase, me_t], tensor=sibling)]
        for k in range(1, nx):
            peer = ((x + k) % nx) * 2 + core
            copies.append(remote(buf.at[me_t], buf.at[me_t], ag_send.at[phase, k], ag_recv.at[phase, me_t], tensor=peer))
        for copy in copies:
            copy.start()
        return copies

    def gather_finish(buf, phase, copies):
        for k in range(1, nx):
            block = ((x + nx - k) % nx) * 2 + core
            remote(buf.at[block], buf.at[block], ag_send.at[phase, nx], ag_recv.at[phase, block], tensor=sibling).wait_recv()
            copy = remote(
                buf.at[block], buf.at[block], ag_send.at[phase, nx - 1 + k], ag_recv.at[phase, block], tensor=sibling
            )
            copy.start()
            copies.append(copy)
        for k in range(nx):
            block = ((x + nx - k) % nx) * 2 + 1 - core
            remote(buf.at[block], buf.at[block], ag_send.at[phase, nx], ag_recv.at[phase, block], tensor=sibling).wait_recv()
        sends.extend(copies)
        return buf[...].reshape(nt * buf.shape[1], width)

    copies = gather_start(full1, 0)

    def path_of(request):
        group = request_group[request]
        return 0, 1 + group_branch[group], 1 + BRANCHES + group

    nodes = path_of(me_s)
    lengths = [node_lengths[n] for n in nodes]
    base = lengths[0] + lengths[1] + lengths[2]
    starts = [0, lengths[0], lengths[0] + lengths[1], base]

    rels = bucket_table.shape[1]
    table = jnp.broadcast_to(bucket_table[...], (8, rels))
    sub = lax.broadcasted_iota(jnp.int32, (8, 1), 0)
    head_bias = jnp.zeros((8, rels), F32)
    for b in range(buckets):
        column = jnp.zeros((8, 1), F32)
        for h in range(heads):
            column = jnp.where(sub == h, rel_weight[h, b], column)
        head_bias = jnp.where(table == b, column, head_bias)
    half = suf // 2
    span = 2 * suf
    for part in range(4):
        first = rels // 2 - suf + 1 + starts[part] - base
        slab = pltpu.roll(head_bias, rels - first, 1)[:, :span]
        for h in range(heads):
            spread = jnp.broadcast_to(slab[h : h + 1, :], (half, span))
            turned = pltpu.roll(spread, span - half + 1, 1, stride=1, stride_axis=0)
            bias[h, part] = turned[:, : span - half]

    @pl.loop(1, ns)
    def _(k):
        peer = seq_from(k)
        remote(kv_in.at[peer], slots.at[peer], seq_send.at[0, k], seq_recv.at[0, peer], seq=peer).wait_recv()

    own_slot.wait()

    path_root[me_s] = slots[node_slot[0]]

    def root_z(k):
        to = y * nz + (z + k) % nz
        return remote(path_root.at[me_s], path_root.at[me_s], z_send.at[k], z_recv.at[z], seq=to)

    def root_y(k):
        row = path_root.at[pl.ds(y * nz, nz)]
        return remote(row, row, y_send.at[k], y_recv.at[y], seq=((y + k) % ny) * nz + z)

    for k in range(1, nz):
        root_z(k).start()

    @pl.loop(1, ns)
    def _(k):
        peer = seq_peer(k)
        for level, node in enumerate(path_of(peer)[1:]):
            kv_send[k, level] = slots[node_slot[node]]
        remote(kv_send.at[k], path_kv.at[:, me_s], seq_send.at[1, k], seq_recv.at[1, me_s], seq=peer).start()

    for level, node in enumerate(nodes[1:]):
        path_kv[level, me_s] = slots[node_slot[node]]

    for k in range(1, nz):
        column = (z + nz - k) % nz
        at = y * nz + column
        remote(path_root.at[at], path_root.at[at], z_send.at[k], z_recv.at[column], seq=at).wait_recv()
    for k in range(1, ny):
        root_y(k).start()

    all_rows = gather_finish(full1, 0, copies)
    for i, (weight, result) in enumerate(((wq, query), (wk, own_key), (wv, own_value))):
        loads[i].wait()
        result[...] = dot(all_rows, weight[...]).astype(BF16)

    @pl.loop(1, ns)
    def _(k):
        peer = seq_from(k)
        remote(kv_send.at[k], path_kv.at[:, peer], seq_send.at[1, k], seq_recv.at[1, peer], seq=peer).wait_recv()

    for k in range(1, ny):
        row = (y + ny - k) % ny
        chunks = path_root.at[pl.ds(row * nz, nz)]
        remote(chunks, chunks, y_send.at[k], y_recv.at[row], seq=row * nz + z).wait_recv()

    lane = lax.broadcasted_iota(jnp.int32, (1, cap), 1)
    penalty = [jnp.where(lane < lengths[level], 0.0, MASKED) for level in range(3)]
    pair_lane = lax.broadcasted_iota(jnp.int32, (1, 128), 1)
    per_pair = 128 // (cols // heads)
    half_chunks = ns // 2
    block_rows = rows // 2

    def attend(part_of):
        firsts = [t * rows + part_of * block_rows for t in range(nt)]
        for pair in range(cols // 128):
            at = slice(pair * 128, pair * 128 + 128)
            paths = (path_root, path_kv.at[0], path_kv.at[1])
            keys = [path[:half_chunks, :, at].reshape(cap, 128) for path in paths] + [own_key[:, at]]
            values = [path[half_chunks:, :, at].reshape(cap, 128) for path in paths] + [own_value[:, at]]
            pair_query = jnp.concatenate([query[f : f + block_rows, at] for f in firsts], axis=0)
            merged = None
            for e in range(per_pair):
                h = pair * per_pair + e
                mine = pair_lane // (128 // per_pair) == e
                head_query = jnp.where(mine, pair_query, jnp.zeros((), BF16))
                scores = []
                for part in range(4):
                    score = lax.dot_general(head_query, keys[part], NT, preferred_element_type=F32)
                    turned = [
                        bias[h, part, f % half : f % half + block_rows, pl.ds(half * (1 - f // half), suf)] for f in firsts
                    ]
                    score = score + jnp.concatenate(turned, axis=0)
                    scores.append(score + penalty[part] if part < 3 else score)
                highest = jnp.maximum(jnp.maximum(scores[0], scores[1]), jnp.maximum(scores[2], scores[3]))
                peak = jnp.max(highest, axis=1, keepdims=True)
                total = None
                summed = None
                for part in range(4):
                    prob = jnp.exp(scores[part] - peak)
                    total = prob if total is None else total + prob
                    term = dot(prob.astype(BF16), values[part])
                    summed = term if summed is None else summed + term
                head_out = summed / jnp.sum(total, axis=1, keepdims=True)
                merged = head_out if merged is None else jnp.where(mine, head_out, merged)
            attn[part_of, :, :, at] = merged.astype(BF16).reshape(nt, block_rows, 128)

    def row_send(row, phase):
        row_out[phase] = row
        for k in range(1, nt):
            peer = (me_t + k) % nt
            send = remote(
                row_out.at[phase], row_in.at[phase, me_t], tail_send.at[phase, k], tail_recv.at[phase, me_t], tensor=peer
            )
            send.start()
            sends.append(send)

    def row_sum(phase):
        row = row_out[phase]
        for k in range(1, nt):
            peer = (me_t + nt - k) % nt
            remote(
                row_out.at[phase], row_in.at[phase, peer], tail_send.at[phase, k], tail_recv.at[phase, peer], tensor=peer
            ).wait_recv()
            row = row + row_in[phase, peer]
        return row

    is_last = me_t == nt - 1

    def last_projected():
        row = dot(attn[1, nt - 1], wo[...])[block_rows - 1 : block_rows]
        row_send(row + jnp.where(is_last, hidden[rows - 1 : rows].astype(F32), 0.0), 0)

    def last_inner():
        row = row_sum(0).astype(BF16).astype(F32)
        left = jnp.broadcast_to(rms_scale(row, ff_gain[...]).astype(F32), (16, width)).astype(BF16)
        inner = (jax.nn.gelu(dot(left, wg[...]), approximate=True) * dot(left, wu[...])).astype(BF16)
        row_send(dot(inner, wd[...])[0:1] + jnp.where(is_last, row, 0.0), 1)

    def last_final():
        last = row_sum(1).astype(BF16).astype(F32)
        mean_square = jnp.mean(last * last, axis=-1, keepdims=True)
        rms = jnp.broadcast_to(jnp.sqrt(mean_square), (1, 128))
        final = (last * lax.rsqrt(mean_square + EPS) * final_gain[...]).astype(BF16).astype(F32)
        for t in range(nt):
            last_send[t] = jnp.concatenate([final[:, t * cols : t * cols + cols], rms], axis=1)

        @pl.loop(1, ns)
        def _(k):
            remote(
                last_send.at[me_t], last_all.at[me_s], seq_send.at[2, k], seq_recv.at[2, me_s], seq=seq_peer(k)
            ).start()

        last_all[me_s] = last_send[me_t]

    per = logit_send.shape[2]
    diagonal = lax.broadcasted_iota(jnp.int32, (ns, 128), 0) == lax.broadcasted_iota(jnp.int32, (ns, 128), 1)

    def last_logits():
        @pl.loop(1, ns)
        def _(k):
            peer = seq_from(k)
            remote(
                last_send.at[me_t], last_all.at[peer], seq_send.at[2, k], seq_recv.at[2, peer], seq=peer
            ).wait_recv()

        lasts = last_all[...].reshape(ns, cols + 128)
        vocab = emb.shape[0]
        logits = lax.dot_general(lasts[:, :cols].astype(BF16), emb[...], NT, preferred_element_type=F32)
        logits = jnp.concatenate([logits, jnp.full((ns, per * nt - vocab), MASKED, F32)], axis=1)
        for t in range(nt):
            logit_send[t] = logits[:, t * per : t * per + per]
        for k in range(1, nt):
            peer = (me_t + k) % nt
            send = remote(logit_send.at[peer], logit_all.at[me_t], tail_send.at[2, k], tail_recv.at[2, me_t], tensor=peer)
            send.start()
            sends.append(send)
        misc[0:1] = jnp.sum(jnp.where(diagonal, lasts[:, cols:], 0.0), axis=0, keepdims=True)

    def top_of_words():
        logit = logit_send[me_t]
        for k in range(1, nt):
            peer = (me_t + nt - k) % nt
            remote(
                logit_send.at[peer], logit_all.at[peer], tail_send.at[2, k], tail_recv.at[2, peer], tensor=peer
            ).wait_recv()
            logit = logit + logit_all[peer]
        highest = jnp.max(logit, axis=1, keepdims=True)
        top_t[me_t] = jnp.max(jnp.where(diagonal, highest, 2 * nt * MASKED), axis=0, keepdims=True)
        for k in range(1, nt):
            peer = (me_t + k) % nt
            send = remote(top_t.at[me_t], top_t.at[me_t], tail_send.at[3, k], tail_recv.at[3, me_t], tensor=peer)
            send.start()
            sends.append(send)

    def top_of_group():
        top = top_t[me_t]
        for k in range(1, nt):
            peer = (me_t + nt - k) % nt
            remote(top_t.at[peer], top_t.at[peer], tail_send.at[3, k], tail_recv.at[3, peer], tensor=peer).wait_recv()
            top = jnp.maximum(top, top_t[peer])
        top_s[me_s] = top

        @pl.loop(1, ns)
        def _(k):
            remote(top_s.at[me_s], top_s.at[me_s], seq_send.at[3, k], seq_recv.at[3, me_s], seq=seq_peer(k)).start()

    def top_of_all():
        @pl.loop(1, ns)
        def _(k):
            peer = seq_from(k)
            remote(top_s.at[peer], top_s.at[peer], seq_send.at[3, k], seq_recv.at[3, peer], seq=peer).wait_recv()

        misc[1:2] = jnp.max(top_s[...].reshape(ns, 128), axis=0, keepdims=True)

    def sum_begin(left, weight, i):
        def product(parity):
            picked = jnp.concatenate([left[2 * k + parity] for k in range(nx)], axis=0)
            return dot(picked, weight[...]).reshape(nx, block_rows, width)

        half_send[i] = product(1 - core).astype(BF16)
        over = remote(half_send.at[i], half_recv.at[i], rs_send.at[i, 0], rs_recv.at[i, nx], tensor=sibling)
        over.start()
        sends.append(over)
        own_sum[i] = product(core)

    others = [2, 1, 3] if nx == 4 else list(range(1, nx))

    def sum_parts(i):
        remote(half_send.at[i], half_recv.at[i], rs_send.at[i, 0], rs_recv.at[i, nx], tensor=sibling).wait_recv()
        for k in others:
            dest = (x + k) % nx
            part_send[i, k] = (own_sum[i, dest] + half_recv[i, dest].astype(F32)).astype(BF16)
            copy = remote(
                part_send.at[i, k], part_recv.at[i, x], rs_send.at[i, k], rs_recv.at[i, x], tensor=dest * 2 + core
            )
            copy.start()
            sends.append(copy)

    def sum_end(i):
        total = own_sum[i, x] + half_recv[i, x].astype(F32)
        for k in others:
            source = (x + nx - k) % nx
            remote(
                part_send.at[i, k], part_recv.at[i, source], rs_send.at[i, k], rs_recv.at[i, source], tensor=sibling
            ).wait_recv()
            total = total + part_recv[i, source].astype(F32)
        return total

    def own_rows(part_of):
        return pl.ds(part_of * block_rows, block_rows)

    def middle(part_of):
        total = sum_end(part_of)
        mid = (hidden[own_rows(part_of)].astype(F32) + total).astype(BF16)
        mids[part_of] = mid
        full2[part_of, me_t] = rms_scale(mid.astype(F32), ff_gain[...])
        return gather_start(full2.at[part_of], 1 + part_of)

    def feed_forward(all_rows, part_of):
        gate = dot(all_rows, wg[...])
        up = dot(all_rows, wu[...])
        inner = (jax.nn.gelu(gate, approximate=True) * up).astype(BF16)
        inner_rows[part_of] = inner.reshape(nt, block_rows, inner.shape[1])

    def finish(part_of):
        out[own_rows(part_of)] = (mids[part_of].astype(F32) + sum_end(2 + part_of)).astype(BF16)

    attend(1)
    for i in range(3, 8):
        loads[i].wait()
    last_projected()
    sum_begin(attn.at[1], wo, 1)
    attend(0)
    sum_parts(1)
    sum_begin(attn.at[0], wo, 0)
    last_inner()
    sum_parts(0)
    copies1 = middle(1)
    last_final()
    copies0 = middle(0)
    feed_forward(gather_finish(full2.at[1], 2, copies1), 1)
    sum_begin(inner_rows.at[1], wd, 3)
    last_logits()
    all_rows = gather_finish(full2.at[0], 1, copies0)
    sum_parts(3)
    feed_forward(all_rows, 0)
    top_of_words()
    sum_begin(inner_rows.at[0], wd, 2)
    sum_parts(2)
    top_of_group()
    finish(1)
    finish(0)

    top_of_all()
    for send in sends:
        send.wait_send()

    @pl.loop(1, ns)
    def _(k):
        peer = seq_peer(k)
        remote(kv_in.at[peer], slots.at[me_s], seq_send.at[0, k], seq_recv.at[0, me_s], seq=peer).wait_send()
        remote(kv_send.at[k], path_kv.at[:, me_s], seq_send.at[1, k], seq_recv.at[1, me_s], seq=peer).wait_send()
        remote(last_send.at[me_t], last_all.at[me_s], seq_send.at[2, k], seq_recv.at[2, me_s], seq=peer).wait_send()
        remote(top_s.at[me_s], top_s.at[me_s], seq_send.at[3, k], seq_recv.at[3, me_s], seq=peer).wait_send()

    for k in range(1, nz):
        root_z(k).wait_send()
    for k in range(1, ny):
        root_y(k).wait_send()


def close(result, misc, out, last_rms, top_logit):
    out[...] = result[...]
    last_rms[...] = misc[0, : last_rms.shape[0]]
    top_logit[...] = misc[1, : top_logit.shape[0]]


def per_device(
    hidden,
    attn_gain,
    attn_query,
    attn_key,
    attn_value,
    attn_out,
    ff_gain,
    ff_gate,
    ff_up,
    ff_down,
    final_gain,
    embedding,
    rel_weight,
    bucket_table,
    prefix_kv,
    node_lengths,
    group_branch,
    node_slot,
    request_group,
):
    ns = lax.axis_size("seq")
    nt = lax.axis_size("tensor")
    nx = nt // 2
    nz = 8 if ns % 8 == 0 else ns
    ny = ns // nz
    rows, width = hidden.shape
    suf = rows * nt
    heads = rel_weight.shape[1]
    cols = attn_query.shape[1]
    cap = prefix_kv.shape[2]
    chunk = 2 * cap // ns
    per = 128 * pl.cdiv(pl.cdiv(embedding.shape[0], nt), 128)
    kv_chunks = prefix_kv.reshape(ns, chunk, cols)
    smem = pl.BlockSpec(memory_space=pltpu.SMEM)
    vmem = pl.BlockSpec(memory_space=pltpu.VMEM)
    hbm = pl.BlockSpec(memory_space=pl.ANY)
    weights = (attn_query, attn_key, attn_value, attn_out, ff_gate, ff_up, ff_down, embedding)
    dma = pltpu.SemaphoreType.DMA
    result, misc = pl.pallas_call(
        functools.partial(kernel, ns, nt),
        out_shape=(jax.ShapeDtypeStruct((rows, width), BF16), jax.ShapeDtypeStruct((8, 128), F32)),
        in_specs=[smem] * 5 + [vmem] * 5 + [hbm] * 9,
        out_specs=(vmem, vmem),
        scratch_shapes=[pltpu.VMEM(w.shape, BF16) for w in weights]
        + [
            pltpu.VMEM((nt, rows, width), BF16),
            pltpu.VMEM((2, nt, rows // 2, width), BF16),
            pltpu.VMEM((ns, chunk, cols), BF16),
            pltpu.VMEM((ns, 2, chunk, cols), BF16),
            pltpu.VMEM((ns, chunk, cols), BF16),
            pltpu.VMEM((2, ns, chunk, cols), BF16),
            pltpu.VMEM((heads, 4, suf // 2, suf + suf // 2), F32),
            pltpu.VMEM((suf, cols), BF16),
            pltpu.VMEM((suf, cols), BF16),
            pltpu.VMEM((suf, cols), BF16),
            pltpu.VMEM((2, nt, rows // 2, cols), BF16),
            pltpu.VMEM((2, nt, rows // 2, ff_down.shape[0]), BF16),
        ]
        + [pltpu.VMEM((4, nx, rows // 2, width), BF16) for _ in range(4)]
        + [
            pltpu.VMEM((4, nx, rows // 2, width), F32),
            pltpu.VMEM((2, rows // 2, width), BF16),
            pltpu.VMEM((nt, 1, cols + 128), F32),
            pltpu.VMEM((2, 1, width), F32),
            pltpu.VMEM((2, nt, 1, width), F32),
            pltpu.VMEM((ns, 1, cols + 128), F32),
            pltpu.VMEM((nt, ns, per), F32),
            pltpu.VMEM((nt, ns, per), F32),
            pltpu.VMEM((nt, 1, 128), F32),
            pltpu.VMEM((ns, 1, 128), F32),
            dma((len(weights) + 1,)),
            dma((3, 2 * nx)),
            dma((3, nt)),
            dma((4, nx)),
            dma((4, nx + 1)),
            dma((4, ns)),
            dma((4, ns)),
            dma((nz,)),
            dma((nz,)),
            dma((ny,)),
            dma((ny,)),
            dma((4, nt)),
            dma((4, nt)),
        ],
        compiler_params=pltpu.CompilerParams(collective_id=0, has_side_effects=True, vmem_limit_bytes=60 << 20),
        name="layer",
    )(
        node_lengths,
        group_branch,
        node_slot,
        request_group,
        rel_weight.T,
        hidden,
        attn_gain.reshape(1, -1),
        ff_gain.reshape(1, -1),
        final_gain.reshape(1, -1),
        bucket_table.reshape(1, -1),
        kv_chunks,
        *weights,
    )
    return pl.pallas_call(
        close,
        out_shape=(
            jax.ShapeDtypeStruct((rows, width), BF16),
            jax.ShapeDtypeStruct((ns,), F32),
            jax.ShapeDtypeStruct((ns,), F32),
        ),
        in_specs=[vmem, vmem],
        out_specs=(vmem, vmem, vmem),
        name="close",
    )(result, misc)


def solution(mesh):
    return jax.shard_map(
        per_device,
        mesh=mesh,
        in_specs=(
            P(("seq", "tensor"), None),
            P(),
            P(None, "tensor"),
            P(None, "tensor"),
            P(None, "tensor"),
            P("tensor", None),
            P(),
            P(None, "tensor"),
            P(None, "tensor"),
            P("tensor", None),
            P(),
            P("seq", "tensor"),
            P(None, "tensor"),
            P(),
            P(None, "seq", None, "tensor"),
            P(),
            P(),
            P(),
            P(),
        ),
        out_specs=(P(("seq", "tensor"), None), P(), P()),
        check_vma=False,
    )
```

```python
import functools

import jax
import jax.numpy as jnp
from jax import lax
from jax.experimental import pallas as pl
from jax.experimental.pallas import tpu as pltpu
from jax.sharding import PartitionSpec as P

MESH = pl.DeviceIdType.MESH
BRANCHES = 7
EPS = 1e-06
MASKED = -1e30
F32 = jnp.float32
BF16 = jnp.bfloat16
NT = (((1,), (1,)), ((), ()))


def remote(src, dst, send_sem, recv_sem, **device):
    return pltpu.make_async_remote_copy(
        src_ref=src, dst_ref=dst, send_sem=send_sem, recv_sem=recv_sem, device_id=device, device_id_type=MESH
    )


def dot(a, b):
    return jnp.dot(a, b, preferred_element_type=F32)


def rms_scale(values, gain):
    mean_square = jnp.mean(values * values, axis=-1, keepdims=True)
    return (values * lax.rsqrt(mean_square + EPS) * gain).astype(BF16)


def kernel(
    ns,
    nt,
    node_lengths,
    group_branch,
    node_slot,
    request_group,
    rel_weight,
    hidden,
    attn_gain,
    ff_gain,
    final_gain,
    bucket_table,
    kv_in,
    wq_in,
    wk_in,
    wv_in,
    wo_in,
    wg_in,
    wu_in,
    wd_in,
    emb_in,
    out,
    misc,
    wq,
    wk,
    wv,
    wo,
    wg,
    wu,
    wd,
    emb,
    full1,
    full2,
    slots,
    kv_send,
    path_root,
    path_kv,
    bias,
    query,
    own_key,
    own_value,
    attn,
    inner_rows,
    half_send,
    half_recv,
    part_send,
    part_recv,
    own_sum,
    mids,
    last_send,
    row_out,
    row_in,
    last_all,
    logit_send,
    logit_all,
    top_t,
    top_s,
    wsem,
    ag_send,
    ag_recv,
    rs_send,
    rs_recv,
    seq_send,
    seq_recv,
    z_send,
    z_recv,
    y_send,
    y_recv,
    tail_send,
    tail_recv,
):
    nx = nt // 2
    nz = 8 if ns % 8 == 0 else ns
    ny = ns // nz
    me_s = lax.axis_index("seq")
    me_t = lax.axis_index("tensor")
    x, core = me_t // 2, me_t % 2
    y, z = me_s // nz, me_s % nz
    sibling = me_t + 1 - 2 * core
    rows, width = hidden.shape
    suf = rows * nt
    heads, buckets = rel_weight.shape
    cols = wq.shape[1]
    chunk = kv_in.shape[1]
    cap = chunk * ns // 2

    sends = []

    def seq_peer(k):
        return ((y + k // nz) % ny) * nz + (z + k % nz) % nz

    def seq_from(k):
        return ((y + ny - k // nz) % ny) * nz + (z + nz - k % nz) % nz

    barrier = pltpu.get_barrier_semaphore()

    @pl.loop(1, ns)
    def _(k):
        pl.semaphore_signal(barrier, inc=1, device_id={"seq": seq_peer(k)}, device_id_type=MESH)

    for k in range(1, nt):
        pl.semaphore_signal(barrier, inc=1, device_id={"tensor": (me_t + k) % nt}, device_id_type=MESH)

    weights = [(wq_in, wq), (wk_in, wk), (wv_in, wv), (wo_in, wo), (wg_in, wg), (wu_in, wu), (wd_in, wd), (emb_in, emb)]
    loads = [pltpu.make_async_copy(a, b, wsem.at[i]) for i, (a, b) in enumerate(weights)]
    own_slot = pltpu.make_async_copy(kv_in.at[me_s], slots.at[me_s], wsem.at[len(weights)])
    own_slot.start()
    for load in loads:
        load.start()

    full1[me_t] = rms_scale(hidden[...].astype(F32), attn_gain[...])
    pl.semaphore_wait(barrier, ns - 1 + nt - 1)

    @pl.loop(1, ns)
    def _(k):
        peer = seq_peer(k)
        remote(kv_in.at[peer], slots.at[me_s], seq_send.at[0, k], seq_recv.at[0, me_s], seq=peer).start()

    def gather_start(buf, phase):
        copies = [remote(buf.at[me_t], buf.at[me_t], ag_send.at[phase, 0], ag_recv.at[phase, me_t], tensor=sibling)]
        for k in range(1, nx):
            peer = ((x + k) % nx) * 2 + core
            copies.append(remote(buf.at[me_t], buf.at[me_t], ag_send.at[phase, k], ag_recv.at[phase, me_t], tensor=peer))
        for copy in copies:
            copy.start()
        return copies

    def gather_finish(buf, phase, copies):
        for k in range(1, nx):
            block = ((x + nx - k) % nx) * 2 + core
            remote(buf.at[block], buf.at[block], ag_send.at[phase, nx], ag_recv.at[phase, block], tensor=sibling).wait_recv()
            copy = remote(
                buf.at[block], buf.at[block], ag_send.at[phase, nx - 1 + k], ag_recv.at[phase, block], tensor=sibling
            )
            copy.start()
            copies.append(copy)
        for k in range(nx):
            block = ((x + nx - k) % nx) * 2 + 1 - core
            remote(buf.at[block], buf.at[block], ag_send.at[phase, nx], ag_recv.at[phase, block], tensor=sibling).wait_recv()
        sends.extend(copies)
        return buf[...].reshape(nt * buf.shape[1], width)

    copies = gather_start(full1, 0)

    def path_of(request):
        group = request_group[request]
        return 0, 1 + group_branch[group], 1 + BRANCHES + group

    nodes = path_of(me_s)
    lengths = [node_lengths[n] for n in nodes]
    base = lengths[0] + lengths[1] + lengths[2]
    starts = [0, lengths[0], lengths[0] + lengths[1], base]

    rels = bucket_table.shape[1]
    table = jnp.broadcast_to(bucket_table[...], (8, rels))
    sub = lax.broadcasted_iota(jnp.int32, (8, 1), 0)
    head_bias = jnp.zeros((8, rels), F32)
    for b in range(buckets):
        column = jnp.zeros((8, 1), F32)
        for h in range(heads):
            column = jnp.where(sub == h, rel_weight[h, b], column)
        head_bias = jnp.where(table == b, column, head_bias)
    half = suf // 2
    span = 2 * suf
    for part in range(4):
        first = rels // 2 - suf + 1 + starts[part] - base
        slab = pltpu.roll(head_bias, rels - first, 1)[:, :span]
        for h in range(heads):
            spread = jnp.broadcast_to(slab[h : h + 1, :], (half, span))
            turned = pltpu.roll(spread, span - half + 1, 1, stride=1, stride_axis=0)
            bias[h, part] = turned[:, : span - half]

    @pl.loop(1, ns)
    def _(k):
        peer = seq_from(k)
        remote(kv_in.at[peer], slots.at[peer], seq_send.at[0, k], seq_recv.at[0, peer], seq=peer).wait_recv()

    own_slot.wait()

    path_root[me_s] = slots[node_slot[0]]

    def root_z(k):
        to = y * nz + (z + k) % nz
        return remote(path_root.at[me_s], path_root.at[me_s], z_send.at[k], z_recv.at[z], seq=to)

    def root_y(k):
        row = path_root.at[pl.ds(y * nz, nz)]
        return remote(row, row, y_send.at[k], y_recv.at[y], seq=((y + k) % ny) * nz + z)

    for k in range(1, nz):
        root_z(k).start()

    @pl.loop(1, ns)
    def _(k):
        peer = seq_peer(k)
        for level, node in enumerate(path_of(peer)[1:]):
            kv_send[k, level] = slots[node_slot[node]]
        remote(kv_send.at[k], path_kv.at[:, me_s], seq_send.at[1, k], seq_recv.at[1, me_s], seq=peer).start()

    for level, node in enumerate(nodes[1:]):
        path_kv[level, me_s] = slots[node_slot[node]]

    for k in range(1, nz):
        column = (z + nz - k) % nz
        at = y * nz + column
        remote(path_root.at[at], path_root.at[at], z_send.at[k], z_recv.at[column], seq=at).wait_recv()
    for k in range(1, ny):
        root_y(k).start()

    all_rows = gather_finish(full1, 0, copies)
    for i, (weight, result) in enumerate(((wq, query), (wk, own_key), (wv, own_value))):
        loads[i].wait()
        result[...] = dot(all_rows, weight[...]).astype(BF16)

    @pl.loop(1, ns)
    def _(k):
        peer = seq_from(k)
        remote(kv_send.at[k], path_kv.at[:, peer], seq_send.at[1, k], seq_recv.at[1, peer], seq=peer).wait_recv()

    for k in range(1, ny):
        row = (y + ny - k) % ny
        chunks = path_root.at[pl.ds(row * nz, nz)]
        remote(chunks, chunks, y_send.at[k], y_recv.at[row], seq=row * nz + z).wait_recv()

    lane = lax.broadcasted_iota(jnp.int32, (1, cap), 1)
    penalty = [jnp.where(lane < lengths[level], 0.0, MASKED) for level in range(3)]
    pair_lane = lax.broadcasted_iota(jnp.int32, (1, 128), 1)
    per_pair = 128 // (cols // heads)
    half_chunks = ns // 2
    block_rows = rows // 2

    def attend(part_of):
        firsts = [t * rows + part_of * block_rows for t in range(nt)]
        for pair in range(cols // 128):
            at = slice(pair * 128, pair * 128 + 128)
            paths = (path_root, path_kv.at[0], path_kv.at[1])
            keys = [path[:half_chunks, :, at].reshape(cap, 128) for path in paths] + [own_key[:, at]]
            values = [path[half_chunks:, :, at].reshape(cap, 128) for path in paths] + [own_value[:, at]]
            pair_query = jnp.concatenate([query[f : f + block_rows, at] for f in firsts], axis=0)
            merged = None
            for e in range(per_pair):
                h = pair * per_pair + e
                mine = pair_lane // (128 // per_pair) == e
                head_query = jnp.where(mine, pair_query, jnp.zeros((), BF16))
                scores = []
                for part in range(4):
                    score = lax.dot_general(head_query, keys[part], NT, preferred_element_type=F32)
                    turned = [
                        bias[h, part, f % half : f % half + block_rows, pl.ds(half * (1 - f // half), suf)] for f in firsts
                    ]
                    score = score + jnp.concatenate(turned, axis=0)
                    scores.append(score + penalty[part] if part < 3 else score)
                highest = jnp.maximum(jnp.maximum(scores[0], scores[1]), jnp.maximum(scores[2], scores[3]))
                peak = jnp.max(highest, axis=1, keepdims=True)
                total = None
                summed = None
                for part in range(4):
                    prob = jnp.exp(scores[part] - peak)
                    total = prob if total is None else total + prob
                    term = dot(prob.astype(BF16), values[part])
                    summed = term if summed is None else summed + term
                head_out = summed / jnp.sum(total, axis=1, keepdims=True)
                merged = head_out if merged is None else jnp.where(mine, head_out, merged)
            attn[part_of, :, :, at] = merged.astype(BF16).reshape(nt, block_rows, 128)

    def row_send(row, phase):
        row_out[phase] = row
        for k in range(1, nt):
            peer = (me_t + k) % nt
            send = remote(
                row_out.at[phase], row_in.at[phase, me_t], tail_send.at[phase, k], tail_recv.at[phase, me_t], tensor=peer
            )
            send.start()
            sends.append(send)

    def row_sum(phase):
        row = row_out[phase]
        for k in range(1, nt):
            peer = (me_t + nt - k) % nt
            remote(
                row_out.at[phase], row_in.at[phase, peer], tail_send.at[phase, k], tail_recv.at[phase, peer], tensor=peer
            ).wait_recv()
            row = row + row_in[phase, peer]
        return row

    is_last = me_t == nt - 1

    def last_projected():
        row = dot(attn[1, nt - 1], wo[...])[block_rows - 1 : block_rows]
        row_send(row + jnp.where(is_last, hidden[rows - 1 : rows].astype(F32), 0.0), 0)

    def last_inner():
        row = row_sum(0).astype(BF16).astype(F32)
        left = jnp.broadcast_to(rms_scale(row, ff_gain[...]).astype(F32), (16, width)).astype(BF16)
        inner = (jax.nn.gelu(dot(left, wg[...]), approximate=True) * dot(left, wu[...])).astype(BF16)
        row_send(dot(inner, wd[...])[0:1] + jnp.where(is_last, row, 0.0), 1)

    def last_final():
        last = row_sum(1).astype(BF16).astype(F32)
        mean_square = jnp.mean(last * last, axis=-1, keepdims=True)
        rms = jnp.broadcast_to(jnp.sqrt(mean_square), (1, 128))
        final = (last * lax.rsqrt(mean_square + EPS) * final_gain[...]).astype(BF16).astype(F32)
        for t in range(nt):
            last_send[t] = jnp.concatenate([final[:, t * cols : t * cols + cols], rms], axis=1)

        @pl.loop(1, ns)
        def _(k):
            remote(
                last_send.at[me_t], last_all.at[me_s], seq_send.at[2, k], seq_recv.at[2, me_s], seq=seq_peer(k)
            ).start()

        last_all[me_s] = last_send[me_t]

    per = logit_send.shape[2]
    diagonal = lax.broadcasted_iota(jnp.int32, (ns, 128), 0) == lax.broadcasted_iota(jnp.int32, (ns, 128), 1)

    def last_logits():
        @pl.loop(1, ns)
        def _(k):
            peer = seq_from(k)
            remote(
                last_send.at[me_t], last_all.at[peer], seq_send.at[2, k], seq_recv.at[2, peer], seq=peer
            ).wait_recv()

        lasts = last_all[...].reshape(ns, cols + 128)
        vocab = emb.shape[0]
        logits = lax.dot_general(lasts[:, :cols].astype(BF16), emb[...], NT, preferred_element_type=F32)
        logits = jnp.concatenate([logits, jnp.full((ns, per * nt - vocab), MASKED, F32)], axis=1)
        for t in range(nt):
            logit_send[t] = logits[:, t * per : t * per + per]
        for k in range(1, nt):
            peer = (me_t + k) % nt
            send = remote(logit_send.at[peer], logit_all.at[me_t], tail_send.at[2, k], tail_recv.at[2, me_t], tensor=peer)
            send.start()
            sends.append(send)
        misc[0:1] = jnp.sum(jnp.where(diagonal, lasts[:, cols:], 0.0), axis=0, keepdims=True)

    def top_of_words():
        logit = logit_send[me_t]
        for k in range(1, nt):
            peer = (me_t + nt - k) % nt
            remote(
                logit_send.at[peer], logit_all.at[peer], tail_send.at[2, k], tail_recv.at[2, peer], tensor=peer
            ).wait_recv()
            logit = logit + logit_all[peer]
        highest = jnp.max(logit, axis=1, keepdims=True)
        top_t[me_t] = jnp.max(jnp.where(diagonal, highest, 2 * nt * MASKED), axis=0, keepdims=True)
        for k in range(1, nt):
            peer = (me_t + k) % nt
            send = remote(top_t.at[me_t], top_t.at[me_t], tail_send.at[3, k], tail_recv.at[3, me_t], tensor=peer)
            send.start()
            sends.append(send)

    def top_of_group():
        top = top_t[me_t]
        for k in range(1, nt):
            peer = (me_t + nt - k) % nt
            remote(top_t.at[peer], top_t.at[peer], tail_send.at[3, k], tail_recv.at[3, peer], tensor=peer).wait_recv()
            top = jnp.maximum(top, top_t[peer])
        top_s[me_s] = top

        @pl.loop(1, ns)
        def _(k):
            remote(top_s.at[me_s], top_s.at[me_s], seq_send.at[3, k], seq_recv.at[3, me_s], seq=seq_peer(k)).start()

    def top_of_all():
        @pl.loop(1, ns)
        def _(k):
            peer = seq_from(k)
            remote(top_s.at[peer], top_s.at[peer], seq_send.at[3, k], seq_recv.at[3, peer], seq=peer).wait_recv()

        misc[1:2] = jnp.max(top_s[...].reshape(ns, 128), axis=0, keepdims=True)

    def sum_begin(left, weight, i):
        def product(parity):
            picked = jnp.concatenate([left[2 * k + parity] for k in range(nx)], axis=0)
            return dot(picked, weight[...]).reshape(nx, block_rows, width)

        half_send[i] = product(1 - core).astype(BF16)
        over = remote(half_send.at[i], half_recv.at[i], rs_send.at[i, 0], rs_recv.at[i, nx], tensor=sibling)
        over.start()
        sends.append(over)
        own_sum[i] = product(core)

    others = [2, 1, 3] if nx == 4 else list(range(1, nx))

    def sum_parts(i):
        remote(half_send.at[i], half_recv.at[i], rs_send.at[i, 0], rs_recv.at[i, nx], tensor=sibling).wait_recv()
        for k in others:
            dest = (x + k) % nx
            part_send[i, k] = (own_sum[i, dest] + half_recv[i, dest].astype(F32)).astype(BF16)
            copy = remote(
                part_send.at[i, k], part_recv.at[i, x], rs_send.at[i, k], rs_recv.at[i, x], tensor=dest * 2 + core
            )
            copy.start()
            sends.append(copy)

    def sum_end(i):
        total = own_sum[i, x] + half_recv[i, x].astype(F32)
        for k in others:
            source = (x + nx - k) % nx
            remote(
                part_send.at[i, k], part_recv.at[i, source], rs_send.at[i, k], rs_recv.at[i, source], tensor=sibling
            ).wait_recv()
            total = total + part_recv[i, source].astype(F32)
        return total

    def own_rows(part_of):
        return pl.ds(part_of * block_rows, block_rows)

    def middle(part_of):
        total = sum_end(part_of)
        mid = (hidden[own_rows(part_of)].astype(F32) + total).astype(BF16)
        mids[part_of] = mid
        full2[part_of, me_t] = rms_scale(mid.astype(F32), ff_gain[...])
        return gather_start(full2.at[part_of], 1 + part_of)

    def feed_forward(all_rows, part_of):
        gate = dot(all_rows, wg[...])
        up = dot(all_rows, wu[...])
        inner = (jax.nn.gelu(gate, approximate=True) * up).astype(BF16)
        inner_rows[part_of] = inner.reshape(nt, block_rows, inner.shape[1])

    def finish(part_of):
        out[own_rows(part_of)] = (mids[part_of].astype(F32) + sum_end(2 + part_of)).astype(BF16)

    def drain(done):
        for send in done:
            send.wait_send()

        @pl.loop(1, ns)
        def _(k):
            peer = seq_peer(k)
            remote(kv_in.at[peer], slots.at[me_s], seq_send.at[0, k], seq_recv.at[0, me_s], seq=peer).wait_send()
            remote(kv_send.at[k], path_kv.at[:, me_s], seq_send.at[1, k], seq_recv.at[1, me_s], seq=peer).wait_send()
            remote(last_send.at[me_t], last_all.at[me_s], seq_send.at[2, k], seq_recv.at[2, me_s], seq=peer).wait_send()

        for k in range(1, nz):
            root_z(k).wait_send()
        for k in range(1, ny):
            root_y(k).wait_send()

    attend(1)
    for i in range(3, 8):
        loads[i].wait()
    last_projected()
    sum_begin(attn.at[1], wo, 1)
    attend(0)
    sum_parts(1)
    sum_begin(attn.at[0], wo, 0)
    last_inner()
    sum_parts(0)
    copies1 = middle(1)
    last_final()
    copies0 = middle(0)
    feed_forward(gather_finish(full2.at[1], 2, copies1), 1)
    sum_begin(inner_rows.at[1], wd, 3)
    last_logits()
    all_rows = gather_finish(full2.at[0], 1, copies0)
    sum_parts(3)
    feed_forward(all_rows, 0)
    top_of_words()
    sum_begin(inner_rows.at[0], wd, 2)
    drained = len(sends)
    sum_parts(2)
    top_of_group()
    drain(sends[:drained])
    finish(1)
    finish(0)

    top_of_all()
    for send in sends[drained:]:
        send.wait_send()

    @pl.loop(1, ns)
    def _(k):
        peer = seq_peer(k)
        remote(top_s.at[me_s], top_s.at[me_s], seq_send.at[3, k], seq_recv.at[3, me_s], seq=peer).wait_send()


def close(result, misc, out, last_rms, top_logit):
    out[...] = result[...]
    last_rms[...] = misc[0, : last_rms.shape[0]]
    top_logit[...] = misc[1, : top_logit.shape[0]]


def per_device(
    hidden,
    attn_gain,
    attn_query,
    attn_key,
    attn_value,
    attn_out,
    ff_gain,
    ff_gate,
    ff_up,
    ff_down,
    final_gain,
    embedding,
    rel_weight,
    bucket_table,
    prefix_kv,
    node_lengths,
    group_branch,
    node_slot,
    request_group,
):
    ns = lax.axis_size("seq")
    nt = lax.axis_size("tensor")
    nx = nt // 2
    nz = 8 if ns % 8 == 0 else ns
    ny = ns // nz
    rows, width = hidden.shape
    suf = rows * nt
    heads = rel_weight.shape[1]
    cols = attn_query.shape[1]
    cap = prefix_kv.shape[2]
    chunk = 2 * cap // ns
    per = 128 * pl.cdiv(pl.cdiv(embedding.shape[0], nt), 128)
    kv_chunks = prefix_kv.reshape(ns, chunk, cols)
    smem = pl.BlockSpec(memory_space=pltpu.SMEM)
    vmem = pl.BlockSpec(memory_space=pltpu.VMEM)
    hbm = pl.BlockSpec(memory_space=pl.ANY)
    weights = (attn_query, attn_key, attn_value, attn_out, ff_gate, ff_up, ff_down, embedding)
    dma = pltpu.SemaphoreType.DMA
    result, misc = pl.pallas_call(
        functools.partial(kernel, ns, nt),
        out_shape=(jax.ShapeDtypeStruct((rows, width), BF16), jax.ShapeDtypeStruct((8, 128), F32)),
        in_specs=[smem] * 5 + [vmem] * 5 + [hbm] * 9,
        out_specs=(vmem, vmem),
        scratch_shapes=[pltpu.VMEM(w.shape, BF16) for w in weights]
        + [
            pltpu.VMEM((nt, rows, width), BF16),
            pltpu.VMEM((2, nt, rows // 2, width), BF16),
            pltpu.VMEM((ns, chunk, cols), BF16),
            pltpu.VMEM((ns, 2, chunk, cols), BF16),
            pltpu.VMEM((ns, chunk, cols), BF16),
            pltpu.VMEM((2, ns, chunk, cols), BF16),
            pltpu.VMEM((heads, 4, suf // 2, suf + suf // 2), F32),
            pltpu.VMEM((suf, cols), BF16),
            pltpu.VMEM((suf, cols), BF16),
            pltpu.VMEM((suf, cols), BF16),
            pltpu.VMEM((2, nt, rows // 2, cols), BF16),
            pltpu.VMEM((2, nt, rows // 2, ff_down.shape[0]), BF16),
        ]
        + [pltpu.VMEM((4, nx, rows // 2, width), BF16) for _ in range(4)]
        + [
            pltpu.VMEM((4, nx, rows // 2, width), F32),
            pltpu.VMEM((2, rows // 2, width), BF16),
            pltpu.VMEM((nt, 1, cols + 128), F32),
            pltpu.VMEM((2, 1, width), F32),
            pltpu.VMEM((2, nt, 1, width), F32),
            pltpu.VMEM((ns, 1, cols + 128), F32),
            pltpu.VMEM((nt, ns, per), F32),
            pltpu.VMEM((nt, ns, per), F32),
            pltpu.VMEM((nt, 1, 128), F32),
            pltpu.VMEM((ns, 1, 128), F32),
            dma((len(weights) + 1,)),
            dma((3, 2 * nx)),
            dma((3, nt)),
            dma((4, nx)),
            dma((4, nx + 1)),
            dma((4, ns)),
            dma((4, ns)),
            dma((nz,)),
            dma((nz,)),
            dma((ny,)),
            dma((ny,)),
            dma((4, nt)),
            dma((4, nt)),
        ],
        compiler_params=pltpu.CompilerParams(collective_id=0, has_side_effects=True, vmem_limit_bytes=60 << 20),
        name="layer",
    )(
        node_lengths,
        group_branch,
        node_slot,
        request_group,
        rel_weight.T,
        hidden,
        attn_gain.reshape(1, -1),
        ff_gain.reshape(1, -1),
        final_gain.reshape(1, -1),
        bucket_table.reshape(1, -1),
        kv_chunks,
        *weights,
    )
    return pl.pallas_call(
        close,
        out_shape=(
            jax.ShapeDtypeStruct((rows, width), BF16),
            jax.ShapeDtypeStruct((ns,), F32),
            jax.ShapeDtypeStruct((ns,), F32),
        ),
        in_specs=[vmem, vmem],
        out_specs=(vmem, vmem, vmem),
        name="close",
    )(result, misc)


def solution(mesh):
    return jax.shard_map(
        per_device,
        mesh=mesh,
        in_specs=(
            P(("seq", "tensor"), None),
            P(),
            P(None, "tensor"),
            P(None, "tensor"),
            P(None, "tensor"),
            P("tensor", None),
            P(),
            P(None, "tensor"),
            P(None, "tensor"),
            P("tensor", None),
            P(),
            P("seq", "tensor"),
            P(None, "tensor"),
            P(),
            P(None, "seq", None, "tensor"),
            P(),
            P(),
            P(),
            P(),
        ),
        out_specs=(P(("seq", "tensor"), None), P(), P()),
        check_vma=False,
    )
```
